128 devices in a mesh: pipe: 2 (over core), dom: 64 (over y, z, x).
Axes of the slice: x: 4, y: 4, z: 4, core: 2. Of those that a mesh axis runs over, the one named last changes fastest.
Arguments:
- node_in: bfloat16 [2, 2, 12288, 512], P('pipe', None, 'dom'), may hold values from -6 to 6
- edge_in: bfloat16 [2, 2, 49152, 512], P('pipe', None, 'dom'), may hold values from -6 to 6
- cot_node: bfloat16 [2, 12288, 512], P(None, 'dom'), may hold values from -6 to 6
- cot_edge: bfloat16 [2, 49152, 512], P(None, 'dom'), may hold values from -6 to 6
- node_count: int32 [64], P('dom'), may hold values from 96 to 192, as said below
- edge_count: int32 [64], P('dom'), may hold values from 1 to 768, as said below
- edge_source: int32 [49152], P('dom'), may hold values from 0 to 319, as said below
- edge_target: int32 [49152], P('dom'), may hold values from 0 to 191, as said below
- halo_send: int32 [64, 64, 2], P('dom'), may hold values from 0 to 191, as said below
- hang_send: int32 [64, 64, 2], P('dom'), may hold values from 0 to 192, as said below
- parent_rows: int32 [64, 64, 2], P('dom'), may hold values from 0 to 192, as said below
- w_edge_in: bfloat16 [2, 1536, 512], P('pipe'), may hold values from -0.15625 to 0.15625
- w_edge_mid: bfloat16 [2, 2, 512, 512], P('pipe'), may hold values from -0.25 to 0.25
- edge_bias: float32 [2, 4, 512], P('pipe'), may hold values from -1.8 to 1.8
- edge_gain: float32 [2, 512], P('pipe'), may hold values from 0.5 to 1.5
- w_node_in: bfloat16 [2, 1024, 512], P('pipe'), may hold values from -0.1875 to 0.1875
- w_node_mid: bfloat16 [2, 2, 512, 512], P('pipe'), may hold values from -0.25 to 0.25
- node_bias: float32 [2, 4, 512], P('pipe'), may hold values from -1.8 to 1.8
- node_gain: float32 [2, 512], P('pipe'), may hold values from 0.5 to 1.5
Outputs:
- grad_node_in: bfloat16 [2, 2, 12288, 512], P('pipe', None, 'dom')
- grad_edge_in: bfloat16 [2, 2, 49152, 512], P('pipe', None, 'dom')
- grad_w_edge_in: float32 [2, 1536, 512], P('pipe', 'dom')
- grad_w_edge_mid: float32 [2, 2, 512, 512], P('pipe', None, 'dom')
- grad_edge_bias: float32 [2, 4, 512], P('pipe', None, 'dom')
- grad_edge_gain: float32 [2, 512], P('pipe', 'dom')
- grad_w_node_in: float32 [2, 1024, 512], P('pipe', 'dom')
- grad_w_node_mid: float32 [2, 2, 512, 512], P('pipe', None, 'dom')
- grad_node_bias: float32 [2, 4, 512], P('pipe', None, 'dom')
- grad_node_gain: float32 [2, 512], P('pipe', 'dom')
The draws below stay inside these ranges and needn't reach their ends.
Inputs may be any that keep to these rules, and one draw needn't show every extreme that they name: Partition p has node_count[p] live node rows; some partition is full. Partition p has edge_count[p] live edge rows; some partition is full. `edge_source`: each edge's source is a live node row of its partition or 192 + k, the k-th received row of its partition. `edge_target`: each edge's target is a live node row of its partition. halo_send[p, q, :] are live rows of partition p. hang_send[p, q, 0] == hang_send[p, q, 1]: a live row of partition p hanging on an edge of partition q, or 192 for none; a row hangs for at most one q, and no hanging row is a parent. parent_rows[q, p, :] are two different live rows of partition q, or both 192 where hang_send[p, q, 0] is 192.
All inputs are finite; a program needn't handle non-finite values.
Results may differ from the reference program's by a relative error of at most 0.015.
Values may be sent and summed in bfloat16 or wider, within the bound.
No kernel may reach another device: no remote copies, remote signals or barrier semaphores. Data moves between devices by JAX's collectives and lax.ppermute only.
A program may use at most 192 MiB of HBM per device.

```python
import jax
import jax.numpy as jnp
from jax import lax

LATENT = 512
NODE_DEV = 192
EDGE_DEV = 768
MICRO = 2
HALO_SLOTS = 2
NODES = 12288
EDGES = 49152
N_DOM = 64


def partition_counts(key):
    node_key, spread_key, jitter_key, full_key, top_key = jax.random.split(jax.random.fold_in(key, 101), 5)
    position = jnp.arange(N_DOM)
    node_total = NODE_DEV // 2 + jax.random.randint(node_key, (N_DOM,), 0, NODE_DEV // 2 + 1)
    fullest = jax.random.randint(full_key, (), 0, N_DOM)
    node_total = jnp.where(position == fullest, NODE_DEV, node_total)
    power = jax.random.randint(spread_key, (N_DOM,), 0, 4)
    base_count = jnp.right_shift(jnp.full((N_DOM,), EDGE_DEV, jnp.int32), power)
    jitter = jax.random.randint(jitter_key, (N_DOM,), 0, 1 << 20) % (base_count // 4 + 1)
    edge_total = base_count - jitter
    busiest = jax.random.randint(top_key, (), 0, N_DOM)
    edge_total = jnp.where(position == busiest, EDGE_DEV, edge_total)
    return (node_total.astype(jnp.int32), edge_total.astype(jnp.int32))


def hanging_lists(key):
    order_key, live_key, pick_key = jax.random.split(jax.random.fold_in(key, 303), 3)
    half_rows = NODE_DEV // 2
    order = jax.vmap(lambda sub: jax.random.permutation(sub, half_rows))(jax.random.split(order_key, N_DOM))
    order = order.astype(jnp.int32)
    live = jax.random.randint(live_key, (N_DOM, N_DOM), 0, 2)
    hanging = order[:, :N_DOM]
    pick = jax.random.randint(pick_key, (N_DOM, N_DOM), N_DOM, half_rows - 1)
    owner = jnp.broadcast_to(jnp.arange(N_DOM)[None, :], (N_DOM, N_DOM))
    first = order[owner, pick]
    second = order[owner, pick + 1]
    sender = jnp.where(live == 1, hanging, NODE_DEV)
    send_rows = jnp.stack([sender, sender], axis=-1)
    parents = jnp.stack([jnp.where(live == 1, first, NODE_DEV), jnp.where(live == 1, second, NODE_DEV)], axis=-1)
    return (send_rows.astype(jnp.int32), jnp.transpose(parents, (1, 0, 2)).astype(jnp.int32))


def draw_node_count(key, part):
    return partition_counts(key)[0]


def draw_edge_count(key, part):
    return partition_counts(key)[1]


def draw_edge_source(key, part):
    node_total = partition_counts(key)[0]
    raw = jax.random.randint(jax.random.fold_in(key, 202), (N_DOM, EDGE_DEV), 0, 1 << 20)
    picked = raw % (node_total[:, None] + N_DOM * HALO_SLOTS)
    source = jnp.where(picked < node_total[:, None], picked, NODE_DEV + picked - node_total[:, None])
    return source.reshape(N_DOM * EDGE_DEV).astype(jnp.int32)


def draw_edge_target(key, part):
    node_total = partition_counts(key)[0]
    raw = jax.random.randint(jax.random.fold_in(key, 212), (N_DOM, EDGE_DEV), 0, 1 << 20)
    return (raw % node_total[:, None]).reshape(N_DOM * EDGE_DEV).astype(jnp.int32)


def draw_halo_send(key, part):
    node_total = partition_counts(key)[0]
    raw = jax.random.randint(jax.random.fold_in(key, 222), (N_DOM, N_DOM, HALO_SLOTS), 0, 1 << 20)
    return (raw % node_total[:, None, None]).astype(jnp.int32)


def draw_hang_send(key, part):
    return hanging_lists(key)[0]


def draw_parent_rows(key, part):
    return hanging_lists(key)[1]


def level_of(rng, shape, cuts, low, high):
    def one(dim, shards_of):
        heights = jax.random.uniform(jax.random.fold_in(jax.random.fold_in(rng, 6), dim), (shards_of,), jnp.float32, low / len(cuts), high / len(cuts))
        return jnp.repeat(jnp.exp(heights), shape[dim] // shards_of).reshape((-1,) + (1,) * (len(shape) - dim - 1))

    loudness = one(*cuts[0])
    for cut in cuts[1:]:
        loudness = loudness * one(*cut)
    return loudness


def bell_draw(rng, extent, spread, bound, cuts=(), kind=jnp.bfloat16):
    array = spread * jax.random.normal(rng, extent, jnp.float32)
    if cuts:
        array = array * level_of(rng, extent, cuts, -0.22, 0.18)
    return jnp.clip(array, -bound, bound).astype(kind)


def setup_inputs(seed: int = 0) -> dict:
    arg_keys = jax.random.split(jax.random.key(seed), 20)
    node_in = bell_draw(arg_keys[0], (2, MICRO, NODES, LATENT), 1.0, 6.0, ((0, 2), (2, 64)))
    edge_in = bell_draw(arg_keys[1], (2, MICRO, EDGES, LATENT), 1.0, 6.0, ((0, 2), (2, 64)))
    cot_node = bell_draw(arg_keys[2], (MICRO, NODES, LATENT), 1.0, 6.0, ((1, 64),))
    cot_edge = bell_draw(arg_keys[3], (MICRO, EDGES, LATENT), 1.0, 6.0, ((1, 64),))
    node_count = draw_node_count(jax.random.fold_in(arg_keys[19], 71), 0)
    edge_count = draw_edge_count(jax.random.fold_in(arg_keys[19], 71), 0)
    edge_source = draw_edge_source(jax.random.fold_in(arg_keys[19], 71), 0)
    edge_target = draw_edge_target(jax.random.fold_in(arg_keys[19], 71), 0)
    halo_send = draw_halo_send(jax.random.fold_in(arg_keys[19], 71), 0)
    hang_send = draw_hang_send(jax.random.fold_in(arg_keys[19], 71), 0)
    parent_rows = draw_parent_rows(jax.random.fold_in(arg_keys[19], 71), 0)
    w_edge_in = bell_draw(arg_keys[11], (2, 3 * LATENT, LATENT), (3 * LATENT) ** -0.5, 0.15625, ((0, 2),))
    w_edge_mid = bell_draw(arg_keys[12], (2, 2, LATENT, LATENT), LATENT ** -0.5, 0.25, ((0, 2),))
    edge_bias = bell_draw(arg_keys[13], (2, 4, LATENT), 0.3, 1.8, ((0, 2),), jnp.float32)
    edge_gain = jnp.clip(1.0 + 0.1 * jax.random.normal(arg_keys[14], (2, LATENT), jnp.float32), 0.5, 1.5)
    w_node_in = bell_draw(arg_keys[15], (2, 2 * LATENT, LATENT), (2 * LATENT) ** -0.5, 0.1875, ((0, 2),))
    w_node_mid = bell_draw(arg_keys[16], (2, 2, LATENT, LATENT), LATENT ** -0.5, 0.25, ((0, 2),))
    node_bias = bell_draw(arg_keys[17], (2, 4, LATENT), 0.3, 1.8, ((0, 2),), jnp.float32)
    node_gain = jnp.clip(1.0 + 0.1 * jax.random.normal(arg_keys[18], (2, LATENT), jnp.float32), 0.5, 1.5)
    return {"node_in": node_in, "edge_in": edge_in, "cot_node": cot_node, "cot_edge": cot_edge, "node_count": node_count, "edge_count": edge_count, "edge_source": edge_source, "edge_target": edge_target, "halo_send": halo_send, "hang_send": hang_send, "parent_rows": parent_rows, "w_edge_in": w_edge_in, "w_edge_mid": w_edge_mid, "edge_bias": edge_bias, "edge_gain": edge_gain, "w_node_in": w_node_in, "w_node_mid": w_node_mid, "node_bias": node_bias, "node_gain": node_gain}


EPS = 1e-05

def silu_slope(value):
    sig = jax.nn.sigmoid(value)
    return sig * (1.0 + value * (1.0 - sig))

def contract_rows(left, right):
    return lax.dot_general(left, right, (((0,), (0,)), ((), ())), preferred_element_type=jnp.float32)

def times_transpose(left, right):
    return lax.dot_general(left, right, (((1,), (1,)), ((), ())), preferred_element_type=jnp.float32)

def mlp_forward(inputs, w_first, w_rest, biases, gains):
    pre_one = jnp.dot(inputs, w_first, preferred_element_type=jnp.float32) + biases[0]
    act_one = jax.nn.silu(pre_one).astype(jnp.bfloat16)
    pre_two = jnp.dot(act_one, w_rest[0], preferred_element_type=jnp.float32) + biases[1]
    act_two = jax.nn.silu(pre_two).astype(jnp.bfloat16)
    pre_out = jnp.dot(act_two, w_rest[1], preferred_element_type=jnp.float32) + biases[2]
    centred = pre_out - lax.optimization_barrier(jnp.mean(pre_out, axis=-1, keepdims=True))
    inv_std = lax.rsqrt(lax.optimization_barrier(jnp.mean(centred * centred, axis=-1, keepdims=True)) + EPS)
    normed = centred * inv_std
    return (normed * gains + biases[3], (pre_one, act_one, pre_two, act_two, normed, inv_std))

def mlp_backward(inputs, grad_out, saved, w_first, w_rest, gains):
    pre_one, act_one, pre_two, act_two, normed, inv_std = saved
    grad_gain = lax.optimization_barrier(jnp.sum(grad_out * normed, axis=0))
    grad_shift = lax.optimization_barrier(jnp.sum(grad_out, axis=0))
    scaled = grad_out * gains
    grad_pre_out = inv_std * (scaled - lax.optimization_barrier(jnp.mean(scaled, axis=-1, keepdims=True)) - normed * lax.optimization_barrier(jnp.mean(scaled * normed, axis=-1, keepdims=True)))
    low_out = grad_pre_out.astype(jnp.bfloat16)
    grad_w_out = contract_rows(act_two, low_out)
    grad_pre_two = times_transpose(low_out, w_rest[1]) * silu_slope(pre_two)
    low_two = grad_pre_two.astype(jnp.bfloat16)
    grad_w_two = contract_rows(act_one, low_two)
    grad_pre_one = times_transpose(low_two, w_rest[0]) * silu_slope(pre_one)
    low_one = grad_pre_one.astype(jnp.bfloat16)
    grad_w_first = contract_rows(inputs, low_one)
    grad_inputs = times_transpose(low_one, w_first)
    grad_biases = jnp.stack([lax.optimization_barrier(jnp.sum(grad_pre_one, axis=0)), lax.optimization_barrier(jnp.sum(grad_pre_two, axis=0)), lax.optimization_barrier(jnp.sum(grad_pre_out, axis=0)), grad_shift])
    return (grad_inputs, grad_w_first, jnp.stack([grad_w_two, grad_w_out]), grad_biases, grad_gain)

def device_backward(nodes, received, edges, source, target, node_total, edge_total, grad_new, grad_edges, params_edge, params_node):
    node_rows = nodes.shape[0]
    latent = nodes.shape[1]
    edge_rows = edges.shape[0]
    extended = jnp.concatenate([nodes, received], 0)
    ext_rows = extended.shape[0]
    edge_live = (jnp.arange(edge_rows) < edge_total).astype(jnp.float32)[:, None]
    node_live = (jnp.arange(node_rows) < node_total).astype(jnp.float32)[:, None]
    features = jnp.concatenate([extended[source], extended[target], edges], 1)
    message, edge_saved = mlp_forward(features, *params_edge)
    gathered = jax.ops.segment_sum(message * edge_live, target, num_segments=node_rows)
    node_input = jnp.concatenate([nodes, gathered.astype(jnp.bfloat16)], 1)
    node_out, node_saved = mlp_forward(node_input, *params_node)
    node_grads = mlp_backward(node_input, grad_new * node_live, node_saved, params_node[0], params_node[1], params_node[3])
    direct = grad_new + node_grads[0][:, :latent]
    grad_agg = node_grads[0][:, latent:]
    upstream = (grad_agg[target] + grad_edges.astype(jnp.float32)) * edge_live
    edge_grads = mlp_backward(features, upstream, edge_saved, params_edge[0], params_edge[1], params_edge[3])
    grad_features = edge_grads[0]
    to_ext = jax.ops.segment_sum(grad_features[:, :latent], source, num_segments=ext_rows) + jax.ops.segment_sum(grad_features[:, latent:2 * latent], target, num_segments=ext_rows)
    edge_result = (grad_edges.astype(jnp.float32) + grad_features[:, 2 * latent:]).astype(jnp.bfloat16)
    local_sum = direct + to_ext[:node_rows]
    return (local_sum, to_ext[node_rows:], edge_result, tuple(edge_grads[1:]) + tuple(node_grads[1:]))

def layer_backward(nodes, edges, grad_nodes, grad_edges, graph, params_edge, params_node):
    source, target, node_total, edge_total, halo_send, hang_send, parent_rows = graph
    peers = N_DOM
    node_rows = NODE_DEV
    latent = LATENT
    flat = nodes.reshape(peers * node_rows, latent)
    owner = jnp.arange(peers, dtype=jnp.int32)[None, :, None]
    pick = (owner * node_rows + jnp.transpose(halo_send, (1, 0, 2))).astype(jnp.int32)
    received = flat[pick.reshape(peers, peers * HALO_SLOTS)]
    padded = jnp.concatenate([grad_nodes, jnp.zeros((peers, 1, latent), jnp.bfloat16)], 1).astype(jnp.float32)
    sent = 0.5 * jax.vmap(lambda rows_all, index: rows_all[index])(padded, hang_send)
    arriving = jnp.transpose(sent, (1, 0, 2, 3)).reshape(peers, peers * 2, latent)
    parent_add = jax.vmap(lambda vals, index: jax.ops.segment_sum(vals, index, num_segments=node_rows + 1)[:node_rows])(arriving, parent_rows.reshape(peers, peers * 2))
    flags = jax.vmap(lambda index: jnp.zeros((node_rows + 1,), jnp.float32).at[index].set(1.0)[:node_rows])(hang_send.reshape(peers, peers * 2))
    grad_new = grad_nodes.astype(jnp.float32) * (1.0 - flags[:, :, None]) + parent_add

    def one_device(carry, items):
        local_sum, halo_part, edge_result, sums = device_backward(*items, params_edge, params_node)
        carry = tuple((older + newer for older, newer in zip(carry, sums)))
        return (carry, (local_sum, halo_part, edge_result))
    init = (jnp.zeros((3 * latent, latent), jnp.float32), jnp.zeros((2, latent, latent), jnp.float32), jnp.zeros((4, latent), jnp.float32), jnp.zeros((latent,), jnp.float32), jnp.zeros((2 * latent, latent), jnp.float32), jnp.zeros((2, latent, latent), jnp.float32), jnp.zeros((4, latent), jnp.float32), jnp.zeros((latent,), jnp.float32))
    sums, outs_all = lax.scan(one_device, init, (nodes, received, edges, source, target, node_total, edge_total, grad_new, grad_edges))
    local_sum, halo_part, edge_result = outs_all
    back = jnp.transpose(halo_part.reshape(peers, peers, HALO_SLOTS, latent), (1, 0, 2, 3)).reshape(peers, peers * HALO_SLOTS, latent)
    returned = jax.vmap(lambda vals, index: jax.ops.segment_sum(vals, index, num_segments=node_rows))(back, halo_send.reshape(peers, peers * HALO_SLOTS))
    node_result = (local_sum + returned).astype(jnp.bfloat16)
    return (node_result, edge_result, sums)

def reference(node_in, edge_in, cot_node, cot_edge, node_count, edge_count, edge_source, edge_target, halo_send, hang_send, parent_rows, w_edge_in, w_edge_mid, edge_bias, edge_gain, w_node_in, w_node_mid, node_bias, node_gain):
    graph = (edge_source.reshape(N_DOM, EDGE_DEV), edge_target.reshape(N_DOM, EDGE_DEV), node_count, edge_count, halo_send, hang_send, parent_rows)
    node_shape = (N_DOM, NODE_DEV, LATENT)
    edge_shape = (N_DOM, EDGE_DEV, LATENT)
    layer_sums = [None, None]
    node_lists = [[], []]
    edge_lists = [[], []]
    for micro_index in range(MICRO):
        grad_nodes = cot_node[micro_index].reshape(node_shape)
        grad_edges = cot_edge[micro_index].reshape(edge_shape)
        for layer in (1, 0):
            params_edge = (w_edge_in[layer], w_edge_mid[layer], edge_bias[layer], edge_gain[layer])
            params_node = (w_node_in[layer], w_node_mid[layer], node_bias[layer], node_gain[layer])
            grad_nodes, grad_edges, sums = layer_backward(node_in[layer, micro_index].reshape(node_shape), edge_in[layer, micro_index].reshape(edge_shape), grad_nodes, grad_edges, graph, params_edge, params_node)
            node_lists[layer].append(grad_nodes.reshape(NODES, LATENT))
            edge_lists[layer].append(grad_edges.reshape(EDGES, LATENT))
            if layer_sums[layer] is None:
                layer_sums[layer] = sums
            else:
                layer_sums[layer] = tuple((older + newer for older, newer in zip(layer_sums[layer], sums)))
    grad_node_in = jnp.stack([jnp.stack(node_lists[0]), jnp.stack(node_lists[1])])
    grad_edge_in = jnp.stack([jnp.stack(edge_lists[0]), jnp.stack(edge_lists[1])])
    stacked = tuple((jnp.stack([first, second]) for first, second in zip(layer_sums[0], layer_sums[1])))
    return (grad_node_in, grad_edge_in, stacked[0], stacked[1], stacked[2], stacked[3], stacked[4], stacked[5], stacked[6], stacked[7])
```

```python
import functools

import jax
import jax.numpy as jnp
from jax import lax
from jax.experimental import pallas as pl
from jax.experimental.pallas import tpu as pltpu
from jax.sharding import PartitionSpec as P

EPS = 1e-05
BF = jnp.bfloat16
F32 = jnp.float32
BLOCK = 256


def dot(a, b):
    return lax.dot_general(a, b, (((1,), (0,)), ((), ())), preferred_element_type=F32)


def dot_t0(a, b):
    return lax.dot_general(a, b, (((0,), (0,)), ((), ())), preferred_element_type=F32)


def dot_t1(a, b):
    return lax.dot_general(a, b, (((1,), (1,)), ((), ())), preferred_element_type=F32)


def hot_rows(index_row, rows):
    grid = lax.broadcasted_iota(jnp.int32, (rows, index_row.shape[1]), 0)
    return jnp.where(grid == index_row, 1.0, 0.0)


def act(value):
    sig = 0.5 * jnp.tanh(0.5 * value) + 0.5
    out = value * sig
    return out.astype(BF), sig + out * (1.0 - sig)


def norm_rows(value):
    centred = value - jnp.mean(value, axis=-1, keepdims=True)
    inv = lax.rsqrt(jnp.mean(centred * centred, axis=-1, keepdims=True) + EPS)
    return centred * inv, inv


def norm_back(grad, gain, normed, inv):
    scaled = grad * gain
    return inv * (
        scaled
        - jnp.mean(scaled, axis=-1, keepdims=True)
        - normed * jnp.mean(scaled * normed, axis=-1, keepdims=True)
    )


def col_sum(value):
    return jnp.sum(value, axis=0, keepdims=True)


def pre_kernel(core, idx, own_all, recv, cot_all, o0, o1, o2, o3, o4, ownb, cotb, sems):
    c = core[0]
    cp = [
        pltpu.make_async_copy(own_all.at[0, c], ownb, sems.at[0]),
        pltpu.make_async_copy(cot_all.at[c], cotb, sems.at[1]),
    ]
    for one in cp:
        one.start()
    rows = ownb.shape[0]
    h0 = hot_rows(idx[0:1, :], rows).astype(BF)
    h1 = hot_rows(idx[1:2, :], rows).astype(BF)
    hg = hot_rows(idx[2:3, :], rows).astype(BF)
    for one in cp:
        one.wait()
    own, other = ownb[...], recv[...]
    low = jnp.where(c == 0, own.astype(F32), other.astype(F32)).astype(BF)
    top = jnp.where(c == 0, other.astype(F32), own.astype(F32)).astype(BF)
    o0[...] = dot_t0(h0, low).astype(BF)
    o1[...] = dot_t0(h1, low).astype(BF)
    o2[...] = dot_t0(h0, top).astype(BF)
    o3[...] = dot_t0(h1, top).astype(BF)
    o4[...] = dot_t0(hg, cotb[...]).astype(BF)


def post_kernel(idx, local, back, node_out, hang_out):
    rows = local.shape[0]
    total = local[...]
    for s in range(2):
        total = total + dot(hot_rows(idx[s : s + 1, :], rows).astype(BF), back[s])
    low = total.astype(BF)
    node_out[...] = low
    hang_out[...] = dot_t0(hot_rows(idx[2:3, :], rows).astype(BF), low).astype(BF)


W_NAMES = 7


def unit_kernel(
    scal, idx, erow, ecol, inc, hang_in,
    own_nodes, own_edges, own_w1, own_wm, own_n1, own_nm, own_vec,
    rec_nodes, rec_edges, rec_w1, rec_wm, rec_n1, rec_nm, rec_vec,
    gout_all, gedge_all,
    local_ref, back_ref, edge_ref, keep_ref, send_ref,
    nodes, edges, w1, wm, n1, nm, vec, gout, gedge,
    oh, q, a1, a2, s1, s2, nrm, inv, msg, l1, l2, l3, gag, bsum, sems,
):
    is_own, c, node_count, edge_count, gi = (scal[i] for i in range(5))
    owns = [own_nodes.at[0, c], own_edges.at[0, c]] + [
        r.at[0] for r in (own_w1, own_wm, own_n1, own_nm)
    ] + [own_vec]
    recs = [rec_nodes, rec_edges, rec_w1, rec_wm, rec_n1, rec_nm, rec_vec]
    dsts = [nodes, edges, w1, wm, n1, nm, vec]
    order = [6, 0, 2, 1, 3, 4, 5]

    @pl.when(is_own == 1)
    def _():
        for k in order:
            pltpu.make_async_copy(owns[k], dsts[k], sems.at[k]).start()

    @pl.when(is_own == 0)
    def _():
        for k in order:
            pltpu.make_async_copy(recs[k], dsts[k], sems.at[k]).start()

    cg = pltpu.make_async_copy(gout_all.at[gi], gout, sems.at[7])
    ce = pltpu.make_async_copy(gedge_all.at[gi], gedge, sems.at[8])
    cg.start()
    ce.start()

    def ready(k):
        pltpu.make_async_copy(recs[k], dsts[k], sems.at[k]).wait()

    n_rows = nodes.shape[0]
    e_rows = edges.shape[0]
    width = nodes.shape[1]
    blocks = e_rows // BLOCK

    def live_of(start, size, count):
        return (lax.broadcasted_iota(jnp.int32, (size, 1), 0) + start < count).astype(F32)

    def build(i, _):
        rows = pl.ds(pl.multiple_of(i * BLOCK, BLOCK), BLOCK)
        grid = lax.broadcasted_iota(jnp.int32, (BLOCK, width), 1)
        hit = (grid == ecol[rows, 0:1]) | (grid == ecol[rows, 1:2])
        oh[rows, :] = jnp.where(hit, 1.0, 0.0).astype(BF)
        return 0

    lax.fori_loop(0, blocks, build, 0)
    ready(6)
    eb = [vec[i : i + 1, :] for i in range(4)]
    eg = vec[4:5, :]
    nb = [vec[i : i + 1, :] for i in range(5, 9)]
    ng = vec[9:10, :]
    ready(0)
    ready(2)
    q[0:n_rows, :] = dot(nodes[...], w1[width : 2 * width, :]).astype(BF)
    q[n_rows : 2 * n_rows, :] = dot(nodes[...], w1[0:width, :]).astype(BF)
    q[2 * n_rows :, :] = dot(inc[...], w1[0:width, :]).astype(BF)
    ready(1)
    ready(3)

    def forward(i, _):
        start = pl.multiple_of(i * BLOCK, BLOCK)
        rows = pl.ds(start, BLOCK)
        z = dot(oh[rows, :], q[...]) + dot(edges[rows, :], w1[2 * width :, :]) + eb[0]
        low, slope = act(z)
        a1[rows, :] = low
        s1[rows, :] = slope
        low, slope = act(dot(low, wm[0]) + eb[1])
        a2[rows, :] = low
        s2[rows, :] = slope
        normed, rstd = norm_rows(dot(low, wm[1]) + eb[2])
        nrm[rows, :] = normed
        inv[rows, :] = rstd
        msg[rows, :] = ((normed * eg + eb[3]) * live_of(start, BLOCK, edge_count)).astype(BF)
        return 0

    lax.fori_loop(0, blocks, forward, 0)

    to_target = hot_rows(erow[1:2, :], n_rows).astype(BF)
    agg = dot(to_target, msg[...]).astype(BF)
    ready(4)
    ready(5)
    x_n = nodes[...]
    na1, ns1 = act(dot(x_n, n1[0:width, :]) + dot(agg, n1[width:, :]) + nb[0])
    na2, ns2 = act(dot(na1, nm[0]) + nb[1])
    nn, nr = norm_rows(dot(na2, nm[1]) + nb[2])

    def halves(low):
        half = width // 2
        f = low.astype(F32)
        swapped = jnp.concatenate([f[:, half:], f[:, :half]], axis=1)
        return jnp.where(c == 0, f, swapped).astype(BF)

    def put(first, pieces):
        half = width // 2
        tile = jnp.concatenate([x.reshape(64, -1, x.shape[-1]) for x in pieces], axis=1)
        n = tile.shape[1]
        keep_ref[:, first : first + n, :] = tile[:, :, :half].astype(BF)
        send_ref[:, first : first + n, :] = tile[:, :, half:].astype(BF)

    cg.wait()
    hung = jnp.max(
        jnp.where(
            lax.broadcasted_iota(jnp.int32, (n_rows, idx.shape[1]), 0) == idx[2:3, :], 1.0, 0.0
        ),
        axis=1,
        keepdims=True,
    )
    spread = 0.5 * (hot_rows(idx[3:4, :], n_rows) + hot_rows(idx[4:5, :], n_rows))
    grad_new = gout[...].astype(F32) * (1.0 - hung) + dot(spread.astype(BF), hang_in[...])
    gy = grad_new * live_of(0, n_rows, node_count)
    bsum[8:9, :] = col_sum(gy)
    bsum[9:10, :] = col_sum(gy * nn)
    g3 = norm_back(gy, ng, nn, nr)
    bsum[7:8, :] = col_sum(g3)
    low3 = g3.astype(BF)
    g2 = dot_t1(low3, nm[1]) * ns2
    bsum[6:7, :] = col_sum(g2)
    low2 = g2.astype(BF)
    g1 = dot_t1(low2, nm[0]) * ns1
    bsum[5:6, :] = col_sum(g1)
    low1 = g1.astype(BF)
    direct = grad_new + dot_t1(low1, n1[0:width, :])
    gag[0:n_rows, :] = dot_t1(low1, n1[width:, :]).astype(BF)
    gag[n_rows:, :] = jnp.zeros((gag.shape[0] - n_rows, width), BF)
    low1p = halves(low1)
    put(48, [jnp.concatenate([dot_t0(x_n, low1p), dot_t0(agg, low1p)], axis=0)])
    put(64, [dot_t0(na1, halves(low2)), dot_t0(na2, halves(low3))])

    ce.wait()
    gk = gag.shape[0]

    def backward(i, carry):
        start = pl.multiple_of(i * BLOCK, BLOCK)
        rows = pl.ds(start, BLOCK)
        c1, c2, c3, c4, c5 = carry
        ge = gedge[rows, :].astype(F32)
        gy = (dot(oh[rows, 0:gk], gag[...]) + ge) * live_of(start, BLOCK, edge_count)
        normed = nrm[rows, :]
        g3 = norm_back(gy, eg, normed, inv[rows, :])
        low = g3.astype(BF)
        l3[rows, :] = halves(low)
        g2 = dot_t1(low, wm[1]) * s2[rows, :]
        low = g2.astype(BF)
        l2[rows, :] = halves(low)
        g1 = dot_t1(low, wm[0]) * s1[rows, :]
        low = g1.astype(BF)
        l1[rows, :] = low
        edge_ref[rows, :] = (ge + dot_t1(low, w1[2 * width :, :])).astype(BF)
        return (
            c1 + col_sum(g1),
            c2 + col_sum(g2),
            c3 + col_sum(g3),
            c4 + col_sum(gy),
            c5 + col_sum(gy * normed),
        )

    zero = jnp.zeros((1, width), F32)
    sums = lax.fori_loop(0, blocks, backward, (zero,) * 5)
    for k in range(5):
        bsum[k : k + 1, :] = sums[k]
    bsum[10:16, :] = jnp.zeros((6, width), F32)

    lowv = l1[...]
    t_sum = dot(to_target, lowv).astype(BF)
    from_source = hot_rows(erow[0:1, :] - n_rows, width - n_rows).astype(BF)
    s_sum = dot(from_source, lowv).astype(BF)
    d_ext = dot_t1(s_sum, w1[0:width, :])
    local_ref[...] = direct + d_ext[0:n_rows, :] + dot_t1(t_sum, w1[width : 2 * width, :])
    per = back_ref.shape[1]
    for s in range(back_ref.shape[0]):
        back_ref[s] = d_ext[n_rows + s * per : n_rows + (s + 1) * per, :].astype(BF)
    sp, tp = halves(s_sum), halves(t_sum)
    grad_w1 = jnp.concatenate(
        [
            dot_t0(x_n, sp[0:n_rows, :]) + dot_t0(inc[...], sp[n_rows:, :]),
            dot_t0(x_n, tp),
            dot_t0(edges[...], halves(lowv)),
        ],
        axis=0,
    )
    groups = []
    for b in range(width // 128):
        cols = slice(b * 128, (b + 1) * 128)
        pair = jnp.concatenate([bsum[0:8, cols], bsum[8:16, cols]], axis=1)
        pair = jnp.concatenate([pair, pair], axis=1)
        groups.append(jnp.broadcast_to(pair[None], (16, 8, width)))
    put(0, [grad_w1, jnp.concatenate(groups, axis=0)])
    put(32, [dot_t0(a1[...], l2[...]), dot_t0(a2[...], l3[...])])


VM = pl.BlockSpec(memory_space=pltpu.VMEM)
SM = pl.BlockSpec(memory_space=pltpu.SMEM)
HB = pl.BlockSpec(memory_space=pl.ANY)


def swap(x):
    return lax.ppermute(x, "pipe", [(0, 1), (1, 0)])


def exchange(x):
    return lax.all_to_all(x, "dom", split_axis=0, concat_axis=0, tiled=True)


def shards(
    node_in, edge_in, cot_node, cot_edge, node_count, edge_count, edge_source, edge_target,
    halo_send, hang_send, parent_rows,
    w_edge_in, w_edge_mid, edge_bias, edge_gain, w_node_in, w_node_mid, node_bias, node_gain,
):
    n_rows, width = node_in.shape[2:]
    e_rows = edge_in.shape[2]
    peers = lax.axis_size("dom")
    slots = halo_send.shape[2]
    c = lax.axis_index("pipe")
    p = lax.axis_index("dom")
    half = width // 2

    vec = jnp.concatenate(
        [edge_bias[0], edge_gain, node_bias[0], node_gain, jnp.zeros((6, width), F32)], axis=0
    )
    pick = functools.partial(lax.dynamic_index_in_dim, keepdims=False)
    rec_nodes = swap(pick(node_in[0], 1 - c))
    rec_edges = swap(pick(edge_in[0], 1 - c))
    rec_vec = swap(vec)
    rec_w1, rec_wm, rec_n1, rec_nm = (
        swap(w[0]) for w in (w_edge_in, w_edge_mid, w_node_in, w_node_mid)
    )

    hs, gs, ps = halo_send[0], hang_send[0], parent_rows[0]
    idx = jnp.stack([hs[:, 0], hs[:, 1], gs[:, 0], ps[:, 0], ps[:, 1]] + [hs[:, 0]] * 3)
    k = edge_source - n_rows
    source = jnp.where(k < 0, edge_source, n_rows + (k % slots) * peers + k // slots)
    ecol = jnp.stack([edge_target, n_rows + source] + [edge_target] * 6, axis=1)
    erow = jnp.stack([n_rows + source, edge_target] + [edge_target] * 6, axis=0)

    row = jax.ShapeDtypeStruct((peers, width), BF)
    outs = pl.pallas_call(
        pre_kernel,
        out_shape=[row] * 5,
        in_specs=[SM, VM, HB, VM, HB],
        out_specs=[VM] * 5,
        scratch_shapes=[
            pltpu.VMEM((n_rows, width), BF),
            pltpu.VMEM((n_rows, width), BF),
            pltpu.SemaphoreType.DMA((2,)),
        ],
        name="pre",
    )(c.reshape(1), idx, node_in, rec_nodes, cot_node)
    got = exchange(jnp.stack(outs, axis=1))
    got = jnp.swapaxes(got, 0, 1)
    inc = [got[0:2].reshape(-1, width), got[2:4].reshape(-1, width)]
    hang_in = got[4]

    chunk_rows = 80
    unit = pl.pallas_call(
        unit_kernel,
        out_shape=[
            jax.ShapeDtypeStruct((n_rows, width), F32),
            jax.ShapeDtypeStruct((slots, peers, width), BF),
            jax.ShapeDtypeStruct((e_rows, width), BF),
            jax.ShapeDtypeStruct((peers, chunk_rows, half), BF),
            jax.ShapeDtypeStruct((peers, chunk_rows, half), BF),
        ],
        in_specs=[SM] + [VM] * 5 + [HB] * 16,
        out_specs=[VM] * 5,
        scratch_shapes=[
            pltpu.VMEM((n_rows, width), BF),
            pltpu.VMEM((e_rows, width), BF),
            pltpu.VMEM(w_edge_in.shape[1:], BF),
            pltpu.VMEM(w_edge_mid.shape[1:], BF),
            pltpu.VMEM(w_node_in.shape[1:], BF),
            pltpu.VMEM(w_node_mid.shape[1:], BF),
            pltpu.VMEM((16, width), F32),
            pltpu.VMEM((n_rows, width), BF),
            pltpu.VMEM((e_rows, width), BF),
            pltpu.VMEM((e_rows, width), BF),
            pltpu.VMEM((width, width), BF),
            pltpu.VMEM((e_rows, width), BF),
            pltpu.VMEM((e_rows, width), BF),
            pltpu.VMEM((e_rows, width), F32),
            pltpu.VMEM((e_rows, width), F32),
            pltpu.VMEM((e_rows, width), F32),
            pltpu.VMEM((e_rows, 1), F32),
            pltpu.VMEM((e_rows, width), BF),
            pltpu.VMEM((e_rows, width), BF),
            pltpu.VMEM((e_rows, width), BF),
            pltpu.VMEM((e_rows, width), BF),
            pltpu.VMEM((256, width), BF),
            pltpu.VMEM((16, width), F32),
            pltpu.SemaphoreType.DMA((9,)),
        ],
        compiler_params=pltpu.CompilerParams(vmem_limit_bytes=56 * 1024 * 1024),
        name="unit",
    )

    def run(layer, inc_l, hang_l, gout, gedge, gi):
        own = (c == layer).astype(jnp.int32)
        scal = jnp.stack([own, c, node_count[0], edge_count[0], gi]).astype(jnp.int32)
        return unit(
            scal, idx, erow, ecol, inc_l, hang_l,
            node_in, edge_in, w_edge_in, w_edge_mid, w_node_in, w_node_mid, vec,
            rec_nodes, rec_edges, rec_w1, rec_wm, rec_n1, rec_nm, rec_vec,
            gout, gedge,
        )

    post = pl.pallas_call(
        post_kernel,
        out_shape=[jax.ShapeDtypeStruct((n_rows, width), BF), row],
        in_specs=[VM] * 3,
        out_specs=[VM] * 2,
        name="post",
    )

    def give_back(local, back):
        came = exchange(jnp.swapaxes(back, 0, 1))
        return post(idx, local, jnp.swapaxes(came, 0, 1))

    def reduced(keep, send):
        mine = (keep.astype(F32) + swap(send).astype(F32)).astype(BF)
        return jnp.sum(exchange(mine).astype(F32), axis=0)

    local1, back1, edge1, keep1, send1 = run(1, inc[1], hang_in, cot_node, cot_edge, c)
    node1, hang1 = give_back(local1, back1)
    hang_in0 = exchange(hang1[:, None, :])[:, 0]
    part1 = reduced(keep1, send1)
    local0, back0, edge0, keep0, send0 = run(
        0, inc[0], hang_in0, node1[None], edge1[None], jnp.zeros((), jnp.int32)
    )
    part0 = reduced(keep0, send0)
    node0, _ = give_back(local0, back0)

    first = c == 0
    up = [(0, 1)]
    down = [(1, 0)]

    def both(r0, r1):
        lower = lax.ppermute(r0, "pipe", down)
        upper = lax.ppermute(r1, "pipe", up)
        return jnp.where(first, jnp.stack([r0, lower]), jnp.stack([upper, r1]))[None]

    node_final = both(node0, node1)
    edge_final = both(edge0, edge1)

    other = swap(jnp.where(first, part1, part0))
    mine = jnp.where(first, part0, part1)
    full = jnp.where(
        first, jnp.concatenate([mine, other], axis=1), jnp.concatenate([other, mine], axis=1)
    )
    bias = jnp.concatenate([mine[24:32, 0:128], mine[24:32, 128:256]], axis=0)
    bias = lax.dynamic_slice_in_dim(bias, (p % 16) * 8, 8, axis=1)
    return (
        node_final,
        edge_final,
        full[None, 0:24],
        jnp.stack([full[32:40], full[40:48]])[None],
        bias[None, 0:4],
        bias[4:5],
        full[None, 48:64],
        jnp.stack([full[64:72], full[72:80]])[None],
        bias[None, 5:9],
        bias[9:10],
    )


def solution(mesh):
    dom3 = P("dom", None, None)
    in_specs = (
        P("pipe", None, "dom", None),
        P("pipe", None, "dom", None),
        P(None, "dom", None),
        P(None, "dom", None),
        P("dom"),
        P("dom"),
        P("dom"),
        P("dom"),
        dom3,
        dom3,
        dom3,
        P("pipe", None, None),
        P("pipe", None, None, None),
        P("pipe", None, None),
        P("pipe", None),
        P("pipe", None, None),
        P("pipe", None, None, None),
        P("pipe", None, None),
        P("pipe", None),
    )
    out_specs = (
        P("pipe", None, "dom", None),
        P("pipe", None, "dom", None),
        P("pipe", "dom", None),
        P("pipe", None, "dom", None),
        P("pipe", None, "dom"),
        P("pipe", "dom"),
        P("pipe", "dom", None),
        P("pipe", None, "dom", None),
        P("pipe", None, "dom"),
        P("pipe", "dom"),
    )
    return jax.shard_map(shards, mesh=mesh, in_specs=in_specs, out_specs=out_specs, check_vma=False)
```

```python
import functools

import jax
import jax.numpy as jnp
from jax import lax
from jax.experimental import pallas as pl
from jax.experimental.pallas import tpu as pltpu
from jax.sharding import PartitionSpec as P

EPS = 1e-05
BF = jnp.bfloat16
F32 = jnp.float32
BLOCK = 256


def dot(a, b):
    return lax.dot_general(a, b, (((1,), (0,)), ((), ())), preferred_element_type=F32)


def dot_t0(a, b):
    return lax.dot_general(a, b, (((0,), (0,)), ((), ())), preferred_element_type=F32)


def dot_t1(a, b):
    return lax.dot_general(a, b, (((1,), (1,)), ((), ())), preferred_element_type=F32)


def hot_rows(index_row, rows):
    grid = lax.broadcasted_iota(jnp.int32, (rows, index_row.shape[1]), 0)
    return jnp.where(grid == index_row, 1.0, 0.0)


def spread_rows(per):
    row = lax.broadcasted_iota(jnp.int32, (8 * per, 4 * per), 0)
    col = lax.broadcasted_iota(jnp.int32, (8 * per, 4 * per), 1)
    return jnp.where(col == (row & 7) * per + (row >> 3), 1.0, 0.0).astype(BF)


def act(value):
    sig = 0.5 * jnp.tanh(0.5 * value) + 0.5
    out = value * sig
    return out.astype(BF), sig + out * (1.0 - sig)


def norm_rows(value):
    centred = value - jnp.mean(value, axis=-1, keepdims=True)
    inv = lax.rsqrt(jnp.mean(centred * centred, axis=-1, keepdims=True) + EPS)
    return centred * inv, inv


def norm_back(grad, gain, normed, inv):
    scaled = grad * gain
    return inv * (
        scaled
        - jnp.mean(scaled, axis=-1, keepdims=True)
        - normed * jnp.mean(scaled * normed, axis=-1, keepdims=True)
    )


def col_sum(value):
    return jnp.sum(value, axis=0, keepdims=True)


def pre_kernel(core, idx, own_all, rec_all, cot_all, out, ownb, recv, cotb, sems):
    c = core[0]
    cp = [
        pltpu.make_async_copy(own_all.at[0, c], ownb, sems.at[0]),
        pltpu.make_async_copy(cot_all.at[c], cotb, sems.at[1]),
        pltpu.make_async_copy(rec_all.at[0, c], recv, sems.at[2]),
    ]
    for one in cp:
        one.start()
    rows = ownb.shape[0]
    h0 = hot_rows(idx[0:1, :], rows).astype(BF)
    h1 = hot_rows(idx[1:2, :], rows).astype(BF)
    hg = hot_rows(idx[2:3, :], rows).astype(BF)
    for one in cp:
        one.wait()
    own, other = ownb[...], recv[...]
    low = jnp.where(c == 0, own.astype(F32), other.astype(F32)).astype(BF)
    top = jnp.where(c == 0, other.astype(F32), own.astype(F32)).astype(BF)
    for k, (hot, rows_of) in enumerate(((h0, low), (h1, low), (h0, top), (h1, top), (hg, cotb[...]))):
        out[k] = dot_t0(hot, rows_of).astype(BF)


def post_kernel(idx, local, back, node_out, hang_out):
    rows = local.shape[0]
    total = local[...]
    for s in range(2):
        total = total + dot(hot_rows(idx[s : s + 1, :], rows).astype(BF), back[s])
    low = total.astype(BF)
    node_out[...] = low
    hang = dot_t0(hot_rows(idx[2:3, :], rows).astype(BF), low).astype(BF)
    half = hang.shape[1] // 2
    hang_out[0] = hang[:, :half]
    hang_out[1] = hang[:, half:]


def sum_kernel(idx, local, came, part_out, node_out):
    per = came.shape[0]
    part_out[...] = jnp.sum(came[:, 0:80, :].astype(F32), axis=0)
    tail = came[:, 80:88, :].astype(F32).reshape(per * 8, came.shape[2]).astype(BF)
    quarters = dot_t0(spread_rows(per), tail).astype(BF)
    rows = local.shape[0]
    total = local[...]
    for s in range(2):
        back = jnp.concatenate(
            [quarters[(s + 2 * k) * per : (s + 2 * k + 1) * per, :] for k in range(2)], axis=1
        )
        total = total + dot(hot_rows(idx[s : s + 1, :], rows).astype(BF), back)
    node_out[...] = total.astype(BF)


def end_kernel(core, p0, p1, r0, r1, n0, n1, m0, m1, node_out, we, wem, wn, wnm):
    def write(left, right, first, second):
        full = jnp.concatenate([left[0:80, :], right[0:80, :]], axis=1)
        node_out[0, 0] = first[...]
        node_out[0, 1] = second[...]
        we[0] = full[0:24, :]
        wem[0, 0] = full[32:40, :]
        wem[0, 1] = full[40:48, :]
        wn[0] = full[48:64, :]
        wnm[0, 0] = full[64:72, :]
        wnm[0, 1] = full[72:80, :]

    @pl.when(core[0] == 0)
    def _():
        write(p0, r0, n0, m0)

    @pl.when(core[0] == 1)
    def _():
        write(r1, p1, m1, n1)


SAVED = 14


def unit_kernel(mode, layer, *refs):
    take = iter(refs)

    def some(n):
        return [next(take) for _ in range(n)]

    forward_part, backward_part = "F" in mode, "B" in mode
    scal, idx, erow, ecol, got = some(5)
    per = got.shape[1]
    inc_of = lambda: jnp.concatenate([got[2 * layer], got[2 * layer + 1]], axis=0)
    hang_in = next(take) if mode == "B" else None
    own_nodes, own_edges, *own_rest = some(7)
    recs = some(7)
    gout_all, gedge_all = some(2) if backward_part else (None, None)
    kept_in = some(SAVED) if mode == "B" else None
    saved = some(SAVED) if mode == "F" else None
    if backward_part:
        local_ref, edge_ref, keep_ref, send_ref = some(4)
        back_ref = next(take) if mode == "FB" else None
    dsts = some(7)
    nodes, edges, w1, wm, n1, nm, vec = dsts
    if mode != "F":
        saved = some(SAVED)
    oh, a1, a2, s1, s2, nrm, inv, _, _, _, _, _, _, _ = saved
    q, msg, gout, gedge, l1, l2, l3, gag, bsum, sems = some(10)

    is_own, c, node_count, edge_count, gi = (scal[i] for i in range(5))
    owns = [own_nodes.at[0, c], own_edges.at[0, c]] + [r.at[0] for r in own_rest[:4]]
    owns = owns + [own_rest[4]]
    recs = [recs[0].at[0, c], recs[1].at[0, c]] + recs[2:]
    order = [6, 0, 2, 1, 3, 4, 5] if forward_part else [6, 0, 5, 4, 3, 2, 1]
    if backward_part:
        cg = pltpu.make_async_copy(gout_all.at[gi], gout, sems.at[7])
        ce = pltpu.make_async_copy(gedge_all.at[gi], gedge, sems.at[8])
    loads = []
    if mode == "B":
        loads = [
            pltpu.make_async_copy(kept_in[k], saved[k], sems.at[9 + k]) for k in range(SAVED)
        ]
        cg.start()
        for k in range(7, SAVED):
            loads[k].start()

    @pl.when(is_own == 1)
    def _():
        for k in order:
            pltpu.make_async_copy(owns[k], dsts[k], sems.at[k]).start()

    @pl.when(is_own == 0)
    def _():
        for k in order:
            pltpu.make_async_copy(recs[k], dsts[k], sems.at[k]).start()

    if mode == "B":
        for k in range(7):
            loads[k].start()
    else:
        if backward_part:
            cg.start()
    if backward_part:
        ce.start()

    def ready(k):
        pltpu.make_async_copy(recs[k], dsts[k], sems.at[k]).wait()

    n_rows = nodes.shape[0]
    e_rows = edges.shape[0]
    width = nodes.shape[1]
    blocks = e_rows // BLOCK

    def live_of(start, size, count):
        return (lax.broadcasted_iota(jnp.int32, (size, 1), 0) + start < count).astype(F32)

    ready(6)
    eb = [vec[i : i + 1, :] for i in range(4)]
    eg = vec[4:5, :]
    nb = [vec[i : i + 1, :] for i in range(5, 9)]
    ng = vec[9:10, :]
    to_target = hot_rows(erow[1:2, :], n_rows).astype(BF)

    if forward_part:
        def build(i, _):
            rows = pl.ds(pl.multiple_of(i * BLOCK, BLOCK), BLOCK)
            grid = lax.broadcasted_iota(jnp.int32, (BLOCK, width), 1)
            hit = (grid == ecol[rows, 0:1]) | (grid == ecol[rows, 1:2])
            oh[rows, :] = jnp.where(hit, 1.0, 0.0).astype(BF)
            return 0

        lax.fori_loop(0, blocks, build, 0)
        ready(0)
        ready(2)
        q[0:n_rows, :] = dot(nodes[...], w1[width : 2 * width, :]).astype(BF)
        q[n_rows : 2 * n_rows, :] = dot(nodes[...], w1[0:width, :]).astype(BF)
        q[2 * n_rows :, :] = dot(inc_of(), w1[0:width, :]).astype(BF)
        ready(1)
        ready(3)

        def forward(i, _):
            start = pl.multiple_of(i * BLOCK, BLOCK)
            rows = pl.ds(start, BLOCK)
            z = dot(oh[rows, :], q[...]) + dot(edges[rows, :], w1[2 * width :, :]) + eb[0]
            low, slope = act(z)
            a1[rows, :] = low
            s1[rows, :] = slope
            low, slope = act(dot(low, wm[0]) + eb[1])
            a2[rows, :] = low
            s2[rows, :] = slope
            normed, rstd = norm_rows(dot(low, wm[1]) + eb[2])
            nrm[rows, :] = normed
            inv[rows, :] = rstd
            msg[rows, :] = ((normed * eg + eb[3]) * live_of(start, BLOCK, edge_count)).astype(BF)
            return 0

        lax.fori_loop(0, blocks, forward, 0)

        agg = dot(to_target, msg[...]).astype(BF)
        ready(4)
        ready(5)
        x_n = nodes[...]
        na1, ns1 = act(dot(x_n, n1[0:width, :]) + dot(agg, n1[width:, :]) + nb[0])
        na2, ns2 = act(dot(na1, nm[0]) + nb[1])
        nn, nr = norm_rows(dot(na2, nm[1]) + nb[2])
        for ref, value in zip(saved[7:], (agg, na1, na2, ns1, ns2, nn, nr)):
            ref[...] = value

    if not backward_part:
        return
    if not forward_part:
        ready(0)
        ready(4)
        ready(5)
        for one in loads[7:]:
            one.wait()
    x_n = nodes[...]
    agg, na1, na2, ns1, ns2, nn, nr = (ref[...] for ref in saved[7:])

    def halves(low):
        half = width // 2
        f = low.astype(F32)
        swapped = jnp.concatenate([f[:, half:], f[:, :half]], axis=1)
        return jnp.where(c == 0, f, swapped).astype(BF)

    def put(first, pieces):
        half = width // 2
        tile = jnp.concatenate([x.reshape(64, -1, x.shape[-1]) for x in pieces], axis=1)
        n = tile.shape[1]
        keep_ref[:, first : first + n, :] = tile[:, :, :half].astype(BF)
        send_ref[:, first : first + n, :] = tile[:, :, half:].astype(BF)

    cg.wait()
    hung = jnp.max(
        jnp.where(
            lax.broadcasted_iota(jnp.int32, (n_rows, idx.shape[1]), 0) == idx[2:3, :], 1.0, 0.0
        ),
        axis=1,
        keepdims=True,
    )
    spread = 0.5 * (hot_rows(idx[3:4, :], n_rows) + hot_rows(idx[4:5, :], n_rows))
    if mode == "B":
        from_hanging = jnp.concatenate([hang_in[0], hang_in[1]], axis=1)
    else:
        from_hanging = got[4]
    grad_new = gout[...].astype(F32) * (1.0 - hung) + dot(spread.astype(BF), from_hanging)
    gy = grad_new * live_of(0, n_rows, node_count)
    bsum[8:9, :] = col_sum(gy)
    bsum[9:10, :] = col_sum(gy * nn)
    g3 = norm_back(gy, ng, nn, nr)
    bsum[7:8, :] = col_sum(g3)
    low3 = g3.astype(BF)
    g2 = dot_t1(low3, nm[1]) * ns2
    bsum[6:7, :] = col_sum(g2)
    low2 = g2.astype(BF)
    g1 = dot_t1(low2, nm[0]) * ns1
    bsum[5:6, :] = col_sum(g1)
    low1 = g1.astype(BF)
    direct = grad_new + dot_t1(low1, n1[0:width, :])
    gag[0:n_rows, :] = dot_t1(low1, n1[width:, :]).astype(BF)
    gag[n_rows:, :] = jnp.zeros((gag.shape[0] - n_rows, width), BF)
    low1p = halves(low1)
    put(48, [jnp.concatenate([dot_t0(x_n, low1p), dot_t0(agg, low1p)], axis=0)])
    put(64, [dot_t0(na1, halves(low2)), dot_t0(na2, halves(low3))])

    if not forward_part:
        ready(1)
        ready(2)
        ready(3)
        for one in loads[:7]:
            one.wait()
    ce.wait()
    gk = gag.shape[0]

    def backward(i, carry):
        start = pl.multiple_of(i * BLOCK, BLOCK)
        rows = pl.ds(start, BLOCK)
        c1, c2, c3, c4, c5 = carry
        ge = gedge[rows, :].astype(F32)
        gy = (dot(oh[rows, 0:gk], gag[...]) + ge) * live_of(start, BLOCK, edge_count)
        normed = nrm[rows, :]
        g3 = norm_back(gy, eg, normed, inv[rows, :])
        low = g3.astype(BF)
        l3[rows, :] = halves(low)
        g2 = dot_t1(low, wm[1]) * s2[rows, :]
        low = g2.astype(BF)
        l2[rows, :] = halves(low)
        g1 = dot_t1(low, wm[0]) * s1[rows, :]
        low = g1.astype(BF)
        l1[rows, :] = low
        edge_ref[rows, :] = (ge + dot_t1(low, w1[2 * width :, :])).astype(BF)
        return (
            c1 + col_sum(g1),
            c2 + col_sum(g2),
            c3 + col_sum(g3),
            c4 + col_sum(gy),
            c5 + col_sum(gy * normed),
        )

    zero = jnp.zeros((1, width), F32)
    sums = lax.fori_loop(0, blocks, backward, (zero,) * 5)
    for k in range(5):
        bsum[k : k + 1, :] = sums[k]
    bsum[10:16, :] = jnp.zeros((6, width), F32)

    lowv = l1[...]
    t_sum = dot(to_target, lowv).astype(BF)
    from_source = hot_rows(erow[0:1, :] - n_rows, width - n_rows).astype(BF)
    s_sum = dot(from_source, lowv).astype(BF)
    d_ext = dot_t1(s_sum, w1[0:width, :])
    local_ref[...] = direct + d_ext[0:n_rows, :] + dot_t1(t_sum, w1[width : 2 * width, :])
    d_inc = d_ext[n_rows:, :].astype(BF)
    if mode == "FB":
        for s in range(back_ref.shape[0]):
            back_ref[s] = d_inc[s * per : (s + 1) * per, :]
    else:
        half = width // 2
        quarters = jnp.concatenate([d_inc[:, :half], d_inc[:, half:]], axis=0)
        rows = dot(spread_rows(per), quarters).reshape(per, 8, half)
        keep_ref[:, 80:88, :] = rows.astype(BF)
        send_ref[:, 80:88, :] = jnp.zeros((per, 8, half), BF)
    sp, tp = halves(s_sum), halves(t_sum)
    grad_w1 = jnp.concatenate(
        [
            dot_t0(x_n, sp[0:n_rows, :]) + dot_t0(inc_of(), sp[n_rows:, :]),
            dot_t0(x_n, tp),
            dot_t0(edges[...], halves(lowv)),
        ],
        axis=0,
    )
    groups = []
    for b in range(width // 128):
        cols = slice(b * 128, (b + 1) * 128)
        pair = jnp.concatenate([bsum[0:8, cols], bsum[8:16, cols]], axis=1)
        pair = jnp.concatenate([pair, pair], axis=1)
        groups.append(jnp.broadcast_to(pair[None], (16, 8, width)))
    put(0, [grad_w1, jnp.concatenate(groups, axis=0)])
    put(32, [dot_t0(a1[...], l2[...]), dot_t0(a2[...], l3[...])])


VM = pl.BlockSpec(memory_space=pltpu.VMEM)
SM = pl.BlockSpec(memory_space=pltpu.SMEM)
HB = pl.BlockSpec(memory_space=pl.ANY)


def swap(x):
    return lax.ppermute(x, "pipe", [(0, 1), (1, 0)])


def exchange(x):
    return lax.all_to_all(x, "dom", split_axis=0, concat_axis=0, tiled=True)


def body(
    node_in, edge_in, cot_node, cot_edge, node_count, edge_count, edge_source, edge_target,
    halo_send, hang_send, parent_rows,
    w_edge_in, w_edge_mid, edge_bias, edge_gain, w_node_in, w_node_mid, node_bias, node_gain,
):
    n_rows, width = node_in.shape[2:]
    e_rows = edge_in.shape[2]
    peers = lax.axis_size("dom")
    slots = halo_send.shape[2]
    c = lax.axis_index("pipe")
    p = lax.axis_index("dom")
    half = width // 2

    vec = jnp.concatenate(
        [edge_bias[0], edge_gain, node_bias[0], node_gain, jnp.zeros((6, width), F32)], axis=0
    )
    rec_nodes = swap(node_in)
    rec_edges = swap(edge_in)
    rec_vec = swap(vec)
    rec_w1, rec_wm, rec_n1, rec_nm = (
        swap(w[0]) for w in (w_edge_in, w_edge_mid, w_node_in, w_node_mid)
    )

    hs, gs, ps = halo_send[0], hang_send[0], parent_rows[0]
    idx = jnp.stack([hs[:, 0], hs[:, 1], gs[:, 0], ps[:, 0], ps[:, 1]] + [hs[:, 0]] * 3)
    k = edge_source - n_rows
    source = jnp.where(k < 0, edge_source, n_rows + (k % slots) * peers + k // slots)
    ecol = jnp.stack([edge_target, n_rows + source] + [edge_target] * 6, axis=1)
    erow = jnp.stack([n_rows + source, edge_target] + [edge_target] * 6, axis=0)

    outs = pl.pallas_call(
        pre_kernel,
        out_shape=jax.ShapeDtypeStruct((5, peers, width), BF),
        in_specs=[SM, VM, HB, HB, HB],
        out_specs=VM,
        scratch_shapes=[
            pltpu.VMEM((n_rows, width), BF),
            pltpu.VMEM((n_rows, width), BF),
            pltpu.VMEM((n_rows, width), BF),
            pltpu.SemaphoreType.DMA((3,)),
        ],
        name="pre",
    )(c.reshape(1), idx, node_in, rec_nodes, cot_node)
    got = exchange(jnp.swapaxes(outs, 0, 1))
    got = jnp.swapaxes(got, 0, 1)

    shape = jax.ShapeDtypeStruct
    saved = [shape((e_rows, width), BF)] * 3 + [shape((e_rows, width), F32)] * 3
    saved += [shape((e_rows, 1), F32)]
    saved += [shape((n_rows, width), BF)] * 3 + [shape((n_rows, width), F32)] * 3
    saved += [shape((n_rows, 1), F32)]

    def results(mode):
        chunk = shape((peers, 80 if mode == "FB" else 88, half), BF)
        some = [shape((n_rows, width), F32), shape((e_rows, width), BF), chunk, chunk]
        return some + ([shape((slots, peers, width), BF)] if mode == "FB" else [])

    stages = [
        shape((n_rows, width), BF),
        shape((e_rows, width), BF),
        shape(w_edge_in.shape[1:], BF),
        shape(w_edge_mid.shape[1:], BF),
        shape(w_node_in.shape[1:], BF),
        shape(w_node_mid.shape[1:], BF),
        shape((16, width), F32),
    ]
    work = [
        shape((width, width), BF),
        shape((e_rows, width), BF),
        shape((n_rows, width), BF),
        shape((e_rows, width), BF),
        shape((e_rows, width), BF),
        shape((e_rows, width), BF),
        shape((e_rows, width), BF),
        shape((256, width), BF),
        shape((16, width), F32),
    ]

    def run(mode, layer, hang_l=None, gout=None, gedge=None, gi=0, kept=()):
        own = (c == layer).astype(jnp.int32)
        scal = jnp.stack([own, c, node_count[0], edge_count[0], jnp.int32(gi)]).astype(jnp.int32)
        back = "B" in mode
        arrays = [scal, idx, erow, ecol, got] + ([hang_l] if mode == "B" else [])
        near = len(arrays) - 1
        arrays += [node_in, edge_in, w_edge_in, w_edge_mid, w_node_in, w_node_mid, vec]
        arrays += [rec_nodes, rec_edges, rec_w1, rec_wm, rec_n1, rec_nm, rec_vec]
        arrays += ([gout, gedge] if back else []) + list(kept)
        outs = (saved if mode == "F" else []) + (results(mode) if back else [])
        scratch = stages + ([] if mode == "F" else saved) + work
        return pl.pallas_call(
            functools.partial(unit_kernel, mode, layer),
            out_shape=outs,
            in_specs=[SM] + [VM] * near + [HB] * (len(arrays) - near - 1),
            out_specs=[VM] * len(outs),
            scratch_shapes=[pltpu.VMEM(x.shape, x.dtype) for x in scratch]
            + [pltpu.SemaphoreType.DMA((9 + SAVED,))],
            compiler_params=pltpu.CompilerParams(vmem_limit_bytes=56 * 1024 * 1024),
        )(*arrays)

    post = pl.pallas_call(
        post_kernel,
        out_shape=[shape((n_rows, width), BF), shape((2, peers, half), BF)],
        in_specs=[VM] * 3,
        out_specs=[VM] * 2,
        name="post",
    )

    def give_back(local, back):
        came = exchange(jnp.swapaxes(back, 0, 1))
        return post(idx, local, jnp.swapaxes(came, 0, 1))

    def paired(keep, send):
        return (keep.astype(F32) + swap(send).astype(F32)).astype(BF)

    local1, edge1, keep1, send1, back1 = run("FB", 1, None, cot_node, cot_edge, c)
    kept0 = run("F", 0)
    node1, hang1 = give_back(local1, back1)
    hang_in0 = exchange(jnp.swapaxes(hang1, 0, 1))
    mine1, hang_in0 = lax.optimization_barrier((paired(keep1, send1), hang_in0))
    part1 = jnp.sum(exchange(mine1).astype(F32), axis=0)
    local0, edge0, keep0, send0 = run(
        "B", 0, jnp.swapaxes(hang_in0, 0, 1), node1[None], edge1[None], 0, kept0
    )
    up = [(0, 1)]
    down = [(1, 0)]
    first = c == 0
    came = exchange(paired(keep0, send0))
    part0, node0 = pl.pallas_call(
        sum_kernel,
        out_shape=[shape((80, half), F32), shape((n_rows, width), BF)],
        in_specs=[VM] * 3,
        out_specs=[VM] * 2,
        name="sums",
    )(idx, local0, came)
    lower = lax.ppermute(edge0, "pipe", down)
    upper = lax.ppermute(edge1, "pipe", up)
    edge_final = jnp.where(first, jnp.stack([edge0, lower]), jnp.stack([upper, edge1]))[None]
    r0, m0 = lax.ppermute((part0, node0), "pipe", down)
    r1, m1 = lax.ppermute((part1, node1), "pipe", up)
    node_final, we, wem, wn, wnm = pl.pallas_call(
        end_kernel,
        out_shape=[
            shape((1, 2, n_rows, width), BF),
            shape((1, 24, width), F32),
            shape((1, 2, 8, width), F32),
            shape((1, 16, width), F32),
            shape((1, 2, 8, width), F32),
        ],
        in_specs=[SM] + [VM] * 8,
        out_specs=[VM] * 5,
        name="end",
    )(c.reshape(1), part0, part1, r0, r1, node0, node1, m0, m1)
    mine = jnp.where(first, part0[24:32], part1[24:32])
    bias = jnp.concatenate([mine[:, 0:128], mine[:, 128:256]], axis=0)
    bias = lax.dynamic_slice_in_dim(bias, (p % 16) * 8, 8, axis=1)
    return (
        node_final,
        edge_final,
        we,
        wem,
        bias[None, 0:4],
        bias[4:5],
        wn,
        wnm,
        bias[None, 5:9],
        bias[9:10],
    )


def solution(mesh):
    dom3 = P("dom", None, None)
    in_specs = (
        P("pipe", None, "dom", None),
        P("pipe", None, "dom", None),
        P(None, "dom", None),
        P(None, "dom", None),
        P("dom"),
        P("dom"),
        P("dom"),
        P("dom"),
        dom3,
        dom3,
        dom3,
        P("pipe", None, None),
        P("pipe", None, None, None),
        P("pipe", None, None),
        P("pipe", None),
        P("pipe", None, None),
        P("pipe", None, None, None),
        P("pipe", None, None),
        P("pipe", None),
    )
    out_specs = (
        P("pipe", None, "dom", None),
        P("pipe", None, "dom", None),
        P("pipe", "dom", None),
        P("pipe", None, "dom", None),
        P("pipe", None, "dom"),
        P("pipe", "dom"),
        P("pipe", "dom", None),
        P("pipe", None, "dom", None),
        P("pipe", None, "dom"),
        P("pipe", "dom"),
    )
    return jax.shard_map(body, mesh=mesh, in_specs=in_specs, out_specs=out_specs, check_vma=False)
```

```python
import functools

import jax
import jax.numpy as jnp
from jax import lax
from jax.experimental import pallas as pl
from jax.experimental.pallas import tpu as pltpu
from jax.sharding import PartitionSpec as P

EPS = 1e-05
BF = jnp.bfloat16
F32 = jnp.float32
BLOCK = 256


def dot(a, b):
    return lax.dot_general(a, b, (((1,), (0,)), ((), ())), preferred_element_type=F32)


def dot_t0(a, b):
    return lax.dot_general(a, b, (((0,), (0,)), ((), ())), preferred_element_type=F32)


def dot_t1(a, b):
    return lax.dot_general(a, b, (((1,), (1,)), ((), ())), preferred_element_type=F32)


def hot_rows(index_row, rows):
    grid = lax.broadcasted_iota(jnp.int32, (rows, index_row.shape[1]), 0)
    return jnp.where(grid == index_row, 1.0, 0.0)


def spread_rows(per, count):
    shape = (8 * per, count * per)
    row = lax.broadcasted_iota(jnp.int32, shape, 0)
    col = lax.broadcasted_iota(jnp.int32, shape, 1)
    return jnp.where(col == (row & 7) * per + (row >> 3), 1.0, 0.0).astype(BF)


def to_chunks(pieces, per):
    count = pieces.shape[0] // per
    rows = dot(spread_rows(per, count), pieces)
    return rows.reshape(per, 8, pieces.shape[1]).astype(BF)


def from_chunks(chunks, count):
    per, _, n = chunks.shape
    rows = chunks.astype(F32).reshape(per * 8, n).astype(BF)
    return dot_t0(spread_rows(per, count), rows).astype(BF)


def fold(rows, per):
    parts = []
    for s in range(rows.shape[0] // per):
        for b in range(rows.shape[1] // 128):
            parts.append(rows[s * per : (s + 1) * per, b * 128 : (b + 1) * 128])
    return jnp.concatenate(parts, axis=0)


def unfold(rows, per):
    return jnp.concatenate([rows[b * per : (b + 1) * per] for b in range(4)], axis=1)


def per_chunk(sums, chunks):
    n = sums.shape[1]
    take = lax.broadcasted_iota(jnp.int32, (128, 16), 0) >> 3
    take = jnp.where(take == lax.broadcasted_iota(jnp.int32, (128, 16), 1), 1.0, 0.0)
    lane = lax.broadcasted_iota(jnp.int32, (128, n), 0)
    col = lax.broadcasted_iota(jnp.int32, (128, n), 1)
    spaced = dot(take.astype(BF), sums.astype(BF))
    spaced = jnp.where((lane & 7) == (col & 7), spaced, 0.0).astype(BF)
    home = lax.broadcasted_iota(jnp.int32, (chunks, n), 1) >> 3
    home = jnp.where(home == lax.broadcasted_iota(jnp.int32, (chunks, n), 0), 1.0, 0.0)
    return dot_t1(home.astype(BF), spaced)


def act(value):
    sig = 0.5 * jnp.tanh(0.5 * value) + 0.5
    out = value * sig
    return out.astype(BF), sig + out * (1.0 - sig)


def norm_rows(value):
    centred = value - jnp.mean(value, axis=-1, keepdims=True)
    inv = lax.rsqrt(jnp.mean(centred * centred, axis=-1, keepdims=True) + EPS)
    return centred * inv, inv


def norm_back(grad, gain, normed, inv):
    scaled = grad * gain
    return inv * (
        scaled
        - jnp.mean(scaled, axis=-1, keepdims=True)
        - normed * jnp.mean(scaled * normed, axis=-1, keepdims=True)
    )


def col_sum(value):
    return jnp.sum(value, axis=0, keepdims=True)


def pre_kernel(
    core, idx, eb, eg, nb, ng, own_all, rec_all, cot_all, out, vec, ownb, recv, cotb, sems
):
    c = core[0]
    cp = [
        pltpu.make_async_copy(own_all.at[0, c], ownb, sems.at[0]),
        pltpu.make_async_copy(cot_all.at[c], cotb, sems.at[1]),
        pltpu.make_async_copy(rec_all.at[0, c], recv, sems.at[2]),
    ]
    for one in cp:
        one.start()
    vec[0:4, :] = eb[0]
    vec[4:5, :] = eg[...]
    vec[5:9, :] = nb[0]
    vec[9:10, :] = ng[...]
    vec[10:16, :] = jnp.zeros((6, vec.shape[1]), F32)
    rows = ownb.shape[0]
    h0, h1, hg = (hot_rows(idx[k : k + 1, :], rows).astype(BF) for k in range(3))
    for one in cp:
        one.wait()
    own, other = ownb[...], recv[...]
    low = jnp.where(c == 0, own.astype(F32), other.astype(F32)).astype(BF)
    top = jnp.where(c == 0, other.astype(F32), own.astype(F32)).astype(BF)
    pairs = ((h0, low), (h1, low), (h0, top), (h1, top), (hg, cotb[...]))
    pieces = jnp.concatenate([dot_t0(hot, src).astype(BF) for hot, src in pairs], axis=0)
    out[...] = to_chunks(pieces, idx.shape[1])


def post_kernel(idx, local, came, node_out, hang_out):
    rows = local.shape[0]
    per = came.shape[0]
    total = local[...]
    back = from_chunks(came[...], 8)
    for s in range(2):
        part = unfold(back[s * 4 * per : (s + 1) * 4 * per], per)
        total = total + dot(hot_rows(idx[s : s + 1, :], rows).astype(BF), part)
    low = total.astype(BF)
    node_out[...] = low
    hang = dot_t0(hot_rows(idx[2:3, :], rows).astype(BF), low).astype(BF)
    hang_out[...] = to_chunks(fold(hang, per), per)


def sum_kernel(idx, local, came, part_out, ship):
    per = came.shape[0]
    half = came.shape[2]
    part = jnp.sum(came[...].astype(F32), axis=0)
    part_out[...] = part
    tail = came[:, 72:80, :].astype(F32).reshape(per * 8, half).astype(BF)
    quarters = dot_t0(spread_rows(per, 5), tail).astype(BF)
    rows = local.shape[0]
    total = local[...]
    for s in range(2):
        back = jnp.concatenate(
            [quarters[(s + 2 * k) * per : (s + 2 * k + 1) * per, :] for k in range(2)], axis=1
        )
        total = total + dot(hot_rows(idx[s : s + 1, :], rows).astype(BF), back)
    ship[0:rows, :] = total.astype(BF)
    split_part(part, ship, rows)


def split_part(part, ship, rows):
    high = part.astype(BF)
    low = (part - high.astype(F32)).astype(BF)
    ship[rows:, :] = jnp.concatenate([high, low], axis=1)


def first_kernel(came, node, part_out, ship):
    rows = node.shape[0]
    part = jnp.sum(came[...].astype(F32), axis=0)
    part = jnp.concatenate([part, jnp.zeros((8, part.shape[1]), F32)], axis=0)
    part_out[...] = part
    ship[0:rows, :] = node[...]
    split_part(part, ship, rows)


def end_kernel(core, p0, p1, s0, s1, r0, r1, node_out, we, wem, wn, wnm):
    def part_of(ship):
        rows = node_out.shape[2]
        half = p0.shape[1]
        return ship[rows:, :half].astype(F32) + ship[rows:, half:].astype(F32)

    def write(left, right, first, second):
        full = jnp.concatenate([left, right], axis=1)
        rows = node_out.shape[2]
        node_out[0, 0] = first[0:rows, :]
        node_out[0, 1] = second[0:rows, :]
        we[0] = full[0:24, :]
        wem[0, 0] = full[24:32, :]
        wem[0, 1] = full[64:72, :]
        wn[0] = full[32:48, :]
        wnm[0, 0] = full[48:56, :]
        wnm[0, 1] = full[56:64, :]

    @pl.when(core[0] == 0)
    def _():
        write(p0[...], part_of(r0), s0, r0)

    @pl.when(core[0] == 1)
    def _():
        write(part_of(r1), p1[...], r1, s1)


SAVED = 14


def unit_kernel(mode, *refs):
    take = iter(refs)

    def some(n):
        return [next(take) for _ in range(n)]

    forward_part, backward_part = "F" in mode, "B" in mode
    scal, idx, erow, ecol, got = some(5)
    per = idx.shape[1]
    hang_in = next(take) if mode == "B" else None
    own_nodes, own_edges, *own_rest = some(7)
    recs = some(7)
    gout_all, gedge_all = some(2) if backward_part else (None, None)
    kept_in = some(SAVED) if mode == "B" else None
    bias_in = next(take) if mode == "B" else None
    saved_out = some(SAVED) if mode == "F" else None
    if backward_part:
        local_ref, edge_out, keep_out, send_out = some(4)
        back_ref, bias_ref, inc_out = some(3) if mode == "FB" else (None, None, None)
    dsts = some(7)
    nodes, edges, w1, wm, n1, nm, vec = dsts
    saved = some(SAVED)
    oh, a1, a2, s1, s2, nrm, inv, _, _, _, _, _, _, _ = saved
    q, msg, gout, gedge, l1, l2, l3, gag, bsum, inc = some(10)
    if backward_part:
        edge_ref, keep_ref, send_ref = some(3)
    sems = next(take)
    sent = []

    def leave(src, dst, sem):
        pltpu.make_async_copy(src, dst, sems.at[sem]).start()

    is_own, c, node_count, edge_count, gi = (scal[i] for i in range(5))
    owns = [own_nodes.at[0, c], own_edges.at[0, c]] + [r.at[0] for r in own_rest[:4]]
    owns = owns + [own_rest[4]]
    recs = [recs[0].at[0, c], recs[1].at[0, c]] + recs[2:]
    if backward_part:
        cg = pltpu.make_async_copy(gout_all.at[gi], gout, sems.at[7])
        ce = pltpu.make_async_copy(gedge_all.at[gi], gedge, sems.at[8])
    loads = []
    if mode == "B":
        loads = [
            pltpu.make_async_copy(kept_in[k], saved[k], sems.at[9 + k]) for k in range(SAVED)
        ]

    def fetch(order):
        @pl.when(is_own == 1)
        def _():
            for k in order:
                pltpu.make_async_copy(owns[k], dsts[k], sems.at[k]).start()

        @pl.when(is_own == 0)
        def _():
            for k in order:
                pltpu.make_async_copy(recs[k], dsts[k], sems.at[k]).start()

    if mode == "B":
        cg.start()
        for k in range(7, SAVED):
            loads[k].start()
        fetch([6, 0, 5, 4])
    else:
        fetch([6, 0, 2, 1, 3])

    def ready(k):
        pltpu.make_async_copy(recs[k], dsts[k], sems.at[k]).wait()

    n_rows = nodes.shape[0]
    e_rows = edges.shape[0]
    width = nodes.shape[1]
    blocks = e_rows // BLOCK

    def live_of(start, size, count):
        return (lax.broadcasted_iota(jnp.int32, (size, 1), 0) + start < count).astype(F32)

    ready(6)
    eb = [vec[i : i + 1, :] for i in range(4)]
    eg = vec[4:5, :]
    nb = [vec[i : i + 1, :] for i in range(5, 9)]
    ng = vec[9:10, :]
    to_target = hot_rows(erow[1:2, :], n_rows).astype(BF)

    if mode == "FB":
        pieces = from_chunks(got[...], 5)
        inc_out[...] = pieces[0 : 2 * per]
        inc[...] = pieces[2 * per : 4 * per]
        from_hanging = pieces[4 * per :]
    else:
        inc[...] = got[...]
        if backward_part:
            from_hanging = unfold(from_chunks(hang_in[...], 4), per)

    if forward_part:
        def build(i, _):
            rows = pl.ds(pl.multiple_of(i * BLOCK, BLOCK), BLOCK)
            grid = lax.broadcasted_iota(jnp.int32, (BLOCK, width), 1)
            hit = (grid == ecol[rows, 0:1]) | (grid == ecol[rows, 1:2])
            oh[rows, :] = jnp.where(hit, 1.0, 0.0).astype(BF)
            return 0

        lax.fori_loop(0, blocks, build, 0)
        ready(0)
        ready(2)
        q[0:n_rows, :] = dot(nodes[...], w1[width : 2 * width, :]).astype(BF)
        q[n_rows : 2 * n_rows, :] = dot(nodes[...], w1[0:width, :]).astype(BF)
        q[2 * n_rows :, :] = dot(inc[...], w1[0:width, :]).astype(BF)
        ready(1)
        ready(3)
        fetch([4, 5])
        if backward_part:
            cg.start()
            ce.start()

        def forward(i, _):
            start = pl.multiple_of(i * BLOCK, BLOCK)
            rows = pl.ds(start, BLOCK)
            z = dot(oh[rows, :], q[...]) + dot(edges[rows, :], w1[2 * width :, :]) + eb[0]
            low, slope = act(z)
            a1[rows, :] = low
            s1[rows, :] = slope
            low, slope = act(dot(low, wm[0]) + eb[1])
            a2[rows, :] = low
            s2[rows, :] = slope
            normed, rstd = norm_rows(dot(low, wm[1]) + eb[2])
            nrm[rows, :] = normed
            inv[rows, :] = rstd
            msg[rows, :] = ((normed * eg + eb[3]) * live_of(start, BLOCK, edge_count)).astype(BF)
            if mode == "F":
                for k in range(7):
                    leave(saved[k].at[rows, :], saved_out[k].at[rows, :], 9 + k)
            return 0

        lax.fori_loop(0, blocks, forward, 0)

        agg = dot(to_target, msg[...]).astype(BF)
        ready(4)
        ready(5)
        x_n = nodes[...]
        na1, ns1 = act(dot(x_n, n1[0:width, :]) + dot(agg, n1[width:, :]) + nb[0])
        na2, ns2 = act(dot(na1, nm[0]) + nb[1])
        nn, nr = norm_rows(dot(na2, nm[1]) + nb[2])
        for ref, value in zip(saved[7:], (agg, na1, na2, ns1, ns2, nn, nr)):
            ref[...] = value

    if not backward_part:
        for k in range(7, SAVED):
            leave(saved[k], saved_out[k], 9 + k)
        for k in range(SAVED):
            pltpu.make_async_copy(saved[k], saved_out[k], sems.at[9 + k]).wait()
        return
    if not forward_part:
        ready(0)
        ready(4)
        ready(5)
        for one in loads[7:]:
            one.wait()
        for one in loads[:7]:
            one.start()
        fetch([3, 2, 1])
        ce.start()
    x_n = nodes[...]
    agg, na1, na2, ns1, ns2, nn, nr = (ref[...] for ref in saved[7:])

    def halves(low):
        half = width // 2
        f = low.astype(F32)
        swapped = jnp.concatenate([f[:, half:], f[:, :half]], axis=1)
        return jnp.where(c == 0, f, swapped).astype(BF)

    def put(first, pieces):
        half = width // 2
        tile = jnp.concatenate([x.reshape(64, -1, x.shape[-1]) for x in pieces], axis=1)
        n = tile.shape[1]
        keep_ref[:, first : first + n, :] = tile[:, :, :half].astype(BF)
        send_ref[:, first : first + n, :] = tile[:, :, half:].astype(BF)
        for ref, dst in ((send_ref, send_out), (keep_ref, keep_out)):
            part = (slice(None), pl.ds(first, n), slice(None))
            copy = pltpu.make_async_copy(ref.at[part], dst.at[part], sems.at[24 + len(sent)])
            copy.start()
            sent.append(copy)

    cg.wait()
    hung = jnp.max(
        jnp.where(
            lax.broadcasted_iota(jnp.int32, (n_rows, idx.shape[1]), 0) == idx[2:3, :], 1.0, 0.0
        ),
        axis=1,
        keepdims=True,
    )
    spread = 0.5 * (hot_rows(idx[3:4, :], n_rows) + hot_rows(idx[4:5, :], n_rows))
    grad_new = gout[...].astype(F32) * (1.0 - hung) + dot(spread.astype(BF), from_hanging)
    gy = grad_new * live_of(0, n_rows, node_count)
    bsum[8:9, :] = col_sum(gy)
    bsum[9:10, :] = col_sum(gy * nn)
    g3 = norm_back(gy, ng, nn, nr)
    bsum[7:8, :] = col_sum(g3)
    low3 = g3.astype(BF)
    g2 = dot_t1(low3, nm[1]) * ns2
    bsum[6:7, :] = col_sum(g2)
    low2 = g2.astype(BF)
    g1 = dot_t1(low2, nm[0]) * ns1
    bsum[5:6, :] = col_sum(g1)
    low1 = g1.astype(BF)
    direct = grad_new + dot_t1(low1, n1[0:width, :])
    gag[0:n_rows, :] = dot_t1(low1, n1[width:, :]).astype(BF)
    gag[n_rows:, :] = jnp.zeros((gag.shape[0] - n_rows, width), BF)
    low1p = halves(low1)
    put(32, [jnp.concatenate([dot_t0(x_n, low1p), dot_t0(agg, low1p)], axis=0)])
    put(48, [dot_t0(na1, halves(low2)), dot_t0(na2, halves(low3))])

    if not forward_part:
        ready(1)
        ready(2)
        ready(3)
        for one in loads[:7]:
            one.wait()
    ce.wait()
    gk = gag.shape[0]

    def backward(i, carry):
        start = pl.multiple_of(i * BLOCK, BLOCK)
        rows = pl.ds(start, BLOCK)
        c1, c2, c3, c4, c5 = carry
        ge = gedge[rows, :].astype(F32)
        gy = (dot(oh[rows, 0:gk], gag[...]) + ge) * live_of(start, BLOCK, edge_count)
        normed = nrm[rows, :]
        g3 = norm_back(gy, eg, normed, inv[rows, :])
        low = g3.astype(BF)
        l3[rows, :] = halves(low)
        g2 = dot_t1(low, wm[1]) * s2[rows, :]
        low = g2.astype(BF)
        l2[rows, :] = halves(low)
        g1 = dot_t1(low, wm[0]) * s1[rows, :]
        low = g1.astype(BF)
        l1[rows, :] = low
        edge_ref[rows, :] = (ge + dot_t1(low, w1[2 * width :, :])).astype(BF)
        leave(edge_ref.at[rows, :], edge_out.at[rows, :], 23)
        return (
            c1 + col_sum(g1),
            c2 + col_sum(g2),
            c3 + col_sum(g3),
            c4 + col_sum(gy),
            c5 + col_sum(gy * normed),
        )

    zero = jnp.zeros((1, width), F32)
    sums = lax.fori_loop(0, blocks, backward, (zero,) * 5)
    for k in range(5):
        bsum[k : k + 1, :] = sums[k]
    bsum[10:16, :] = jnp.zeros((6, width), F32)

    lowv = l1[...]
    t_sum = dot(to_target, lowv).astype(BF)
    from_source = hot_rows(erow[0:1, :] - n_rows, width - n_rows).astype(BF)
    s_sum = dot(from_source, lowv).astype(BF)
    d_ext = dot_t1(s_sum, w1[0:width, :])
    local_ref[...] = direct + d_ext[0:n_rows, :] + dot_t1(t_sum, w1[width : 2 * width, :])
    d_inc = d_ext[n_rows:, :].astype(BF)
    bias_row = per_chunk(bsum[...], per)
    half = width // 2
    extra = []
    if mode == "FB":
        back_ref[...] = to_chunks(fold(d_inc, per), per)
        bias_ref[...] = bias_row
    else:
        bias_row = jnp.concatenate([bias_row, bias_in[...]], axis=1).astype(BF)
        kept = jnp.concatenate([d_inc[:, :half], d_inc[:, half:], bias_row], axis=0)
        given = jnp.concatenate([jnp.zeros((4 * per, half), BF), bias_row], axis=0)
        place = spread_rows(per, 5)
        extra = [jnp.concatenate([dot(place, kept), dot(place, given)], axis=1)]
    put(64, [dot_t0(a2[...], l3[...])] + extra)
    sp, tp = halves(s_sum), halves(t_sum)
    grad_w1 = jnp.concatenate(
        [
            dot_t0(x_n, sp[0:n_rows, :]) + dot_t0(inc[...], sp[n_rows:, :]),
            dot_t0(x_n, tp),
            dot_t0(edges[...], halves(lowv)),
        ],
        axis=0,
    )
    put(0, [grad_w1, dot_t0(a1[...], l2[...])])
    for copy in sent:
        copy.wait()
    pltpu.make_async_copy(edge_ref, edge_out, sems.at[23]).wait()


VM = pl.BlockSpec(memory_space=pltpu.VMEM)
SM = pl.BlockSpec(memory_space=pltpu.SMEM)
HB = pl.BlockSpec(memory_space=pl.ANY)


def swap(x):
    return lax.ppermute(x, "pipe", [(0, 1), (1, 0)])


def exchange(x):
    return lax.all_to_all(x, "dom", split_axis=0, concat_axis=0, tiled=True)


def body(
    node_in, edge_in, cot_node, cot_edge, node_count, edge_count, edge_source, edge_target,
    halo_send, hang_send, parent_rows,
    w_edge_in, w_edge_mid, edge_bias, edge_gain, w_node_in, w_node_mid, node_bias, node_gain,
):
    n_rows, width = node_in.shape[2:]
    e_rows = edge_in.shape[2]
    peers = lax.axis_size("dom")
    slots = halo_send.shape[2]
    c = lax.axis_index("pipe")
    half = width // 2

    rec_nodes = swap(node_in)

    hs, gs, ps = halo_send[0], hang_send[0], parent_rows[0]
    idx = jnp.stack([hs[:, 0], hs[:, 1], gs[:, 0], ps[:, 0], ps[:, 1]] + [hs[:, 0]] * 3)
    k = edge_source - n_rows
    source = jnp.where(k < 0, edge_source, n_rows + (k % slots) * peers + k // slots)
    ecol = jnp.stack([edge_target, n_rows + source] + [edge_target] * 6, axis=1)
    erow = jnp.stack([n_rows + source, edge_target] + [edge_target] * 6, axis=0)

    rec_nodes, idx = lax.optimization_barrier((rec_nodes, idx))
    outs, vec = pl.pallas_call(
        pre_kernel,
        out_shape=[
            jax.ShapeDtypeStruct((peers, 8, width), BF),
            jax.ShapeDtypeStruct((16, width), F32),
        ],
        in_specs=[SM] + [VM] * 5 + [HB] * 3,
        out_specs=[VM] * 2,
        scratch_shapes=[pltpu.VMEM((n_rows, width), BF)] * 3 + [pltpu.SemaphoreType.DMA((3,))],
        name="pre",
    )(
        c.reshape(1), idx, edge_bias, edge_gain, node_bias, node_gain,
        node_in, rec_nodes, cot_node,
    )
    rec_vec = swap(vec)
    bulk = (edge_in, w_edge_in, w_edge_mid, w_node_in, w_node_mid)
    bulk, _ = lax.optimization_barrier((bulk, rec_nodes))
    rec_edges = swap(bulk[0])
    rec_w1, rec_wm, rec_n1, rec_nm = (swap(w[0]) for w in bulk[1:])
    got = exchange(outs)

    shape = jax.ShapeDtypeStruct
    saved = [shape((e_rows, width), BF)] * 3 + [shape((e_rows, width), F32)] * 3
    saved += [shape((e_rows, 1), F32)]
    saved += [shape((n_rows, width), BF)] * 3 + [shape((n_rows, width), F32)] * 3
    saved += [shape((n_rows, 1), F32)]

    def results(mode):
        chunk = shape((peers, 72 if mode == "FB" else 80, half), BF)
        some = [shape((n_rows, width), F32), shape((e_rows, width), BF), chunk, chunk]
        if mode == "FB":
            some += [shape((peers, 8, 128), BF), shape((peers, 128), F32)]
            some += [shape((slots * peers, width), BF)]
        return some

    stages = [
        shape((n_rows, width), BF),
        shape((e_rows, width), BF),
        shape(w_edge_in.shape[1:], BF),
        shape(w_edge_mid.shape[1:], BF),
        shape(w_node_in.shape[1:], BF),
        shape(w_node_mid.shape[1:], BF),
        shape((16, width), F32),
    ]
    work = [
        shape((width, width), BF),
        shape((e_rows, width), BF),
        shape((n_rows, width), BF),
        shape((e_rows, width), BF),
        shape((e_rows, width), BF),
        shape((e_rows, width), BF),
        shape((e_rows, width), BF),
        shape((256, width), BF),
        shape((16, width), F32),
        shape((slots * peers, width), BF),
    ]

    def run(mode, layer, got, hang_l=None, gout=None, gedge=None, gi=0, kept=(), bias=()):
        own = (c == layer).astype(jnp.int32)
        scal = jnp.stack([own, c, node_count[0], edge_count[0], jnp.int32(gi)]).astype(jnp.int32)
        back = "B" in mode
        arrays = [scal, idx, erow, ecol, got] + ([hang_l] if mode == "B" else [])
        near = len(arrays) - 1
        arrays += [node_in, edge_in, w_edge_in, w_edge_mid, w_node_in, w_node_mid, vec]
        arrays += [rec_nodes, rec_edges, rec_w1, rec_wm, rec_n1, rec_nm, rec_vec]
        arrays += ([gout, gedge] if back else []) + list(kept)
        far = len(arrays)
        arrays += list(bias)
        outs = (saved if mode == "F" else []) + (results(mode) if back else [])
        scratch = stages + saved + work + (results(mode)[1:4] if back else [])
        out_specs = [HB] * len(outs)
        if back:
            out_specs = [VM, HB, HB, HB] + [VM] * (len(outs) - 4)
        return pl.pallas_call(
            functools.partial(unit_kernel, mode),
            out_shape=outs,
            in_specs=[SM] + [VM] * near + [HB] * (far - near - 1) + [VM] * len(bias),
            out_specs=out_specs,
            scratch_shapes=[pltpu.VMEM(x.shape, x.dtype) for x in scratch]
            + [pltpu.SemaphoreType.DMA((40,))],
            compiler_params=pltpu.CompilerParams(vmem_limit_bytes=56 * 1024 * 1024),
        )(*arrays)

    post = pl.pallas_call(
        post_kernel,
        out_shape=[shape((n_rows, width), BF), shape((peers, 8, 128), BF)],
        in_specs=[VM] * 3,
        out_specs=[VM] * 2,
        name="post",
    )

    def paired(keep, send):
        return (keep.astype(F32) + swap(send).astype(F32)).astype(BF)

    local1, edge1, keep1, send1, back1, bias1, inc0 = run("FB", 1, got, None, cot_node, cot_edge, c)
    kept0 = run("F", 0, inc0)
    node1, hang1 = post(idx, local1, exchange(back1))
    hang_in0 = exchange(hang1)
    mine1, hang_in0 = lax.optimization_barrier((paired(keep1, send1), hang_in0))
    came1 = exchange(mine1)
    local0, edge0, keep0, send0 = run(
        "B", 0, inc0, hang_in0, node1[None], edge1[None], 0, kept0, [bias1]
    )
    up = [(0, 1)]
    down = [(1, 0)]
    first = c == 0
    came0 = exchange(paired(keep0, send0))
    sums_out = [shape((80, half), F32), shape((n_rows + 80, width), BF)]
    part1, ship1 = pl.pallas_call(
        first_kernel,
        out_shape=sums_out,
        in_specs=[VM] * 2,
        out_specs=[VM] * 2,
        name="sums1",
    )(came1, node1)
    part0, ship0 = pl.pallas_call(
        sum_kernel,
        out_shape=sums_out,
        in_specs=[VM] * 3,
        out_specs=[VM] * 2,
        name="sums0",
    )(idx, local0, came0)
    lower = lax.ppermute(edge0, "pipe", down)
    upper = lax.ppermute(edge1, "pipe", up)
    edge_final = jnp.where(first, jnp.stack([edge0, lower]), jnp.stack([upper, edge1]))[None]
    r0 = lax.ppermute(ship0, "pipe", down)
    r1 = lax.ppermute(ship1, "pipe", up)
    node_final, we, wem, wn, wnm = pl.pallas_call(
        end_kernel,
        out_shape=[
            shape((1, 2, n_rows, width), BF),
            shape((1, 24, width), F32),
            shape((1, 2, 8, width), F32),
            shape((1, 16, width), F32),
            shape((1, 2, 8, width), F32),
        ],
        in_specs=[SM] + [VM] * 6,
        out_specs=[VM] * 5,
        name="end",
    )(c.reshape(1), part0, part1, ship0, ship1, r0, r1)
    bias = jnp.where(first, part0[76, 0:128], part0[76, 128:256]).reshape(16, 8)
    return (
        node_final,
        edge_final,
        we,
        wem,
        bias[None, 0:4],
        bias[4:5],
        wn,
        wnm,
        bias[None, 5:9],
        bias[9:10],
    )


def solution(mesh):
    dom3 = P("dom", None, None)
    in_specs = (
        P("pipe", None, "dom", None),
        P("pipe", None, "dom", None),
        P(None, "dom", None),
        P(None, "dom", None),
        P("dom"),
        P("dom"),
        P("dom"),
        P("dom"),
        dom3,
        dom3,
        dom3,
        P("pipe", None, None),
        P("pipe", None, None, None),
        P("pipe", None, None),
        P("pipe", None),
        P("pipe", None, None),
        P("pipe", None, None, None),
        P("pipe", None, None),
        P("pipe", None),
    )
    out_specs = (
        P("pipe", None, "dom", None),
        P("pipe", None, "dom", None),
        P("pipe", "dom", None),
        P("pipe", None, "dom", None),
        P("pipe", None, "dom"),
        P("pipe", "dom"),
        P("pipe", "dom", None),
        P("pipe", None, "dom", None),
        P("pipe", None, "dom"),
        P("pipe", "dom"),
    )
    return jax.shard_map(body, mesh=mesh, in_specs=in_specs, out_specs=out_specs, check_vma=False)
```

```python
import functools

import jax
import jax.numpy as jnp
from jax import lax
from jax.experimental import pallas as pl
from jax.experimental.pallas import tpu as pltpu
from jax.sharding import PartitionSpec as P

EPS = 1e-05
BF = jnp.bfloat16
F32 = jnp.float32


def dot(a, b):
    return lax.dot_general(a, b, (((1,), (0,)), ((), ())), preferred_element_type=F32)


def dot_t0(a, b):
    return lax.dot_general(a, b, (((0,), (0,)), ((), ())), preferred_element_type=F32)


def dot_t1(a, b):
    return lax.dot_general(a, b, (((1,), (1,)), ((), ())), preferred_element_type=F32)


def hot_rows(index_row, rows):
    grid = lax.broadcasted_iota(jnp.int32, (rows, index_row.shape[1]), 0)
    return jnp.where(grid == index_row, 1.0, 0.0)


def spread_rows(per, count):
    shape = (8 * per, count * per)
    row = lax.broadcasted_iota(jnp.int32, shape, 0)
    col = lax.broadcasted_iota(jnp.int32, shape, 1)
    return jnp.where(col == (row & 7) * per + (row >> 3), 1.0, 0.0).astype(BF)


def to_chunks(pieces, per):
    count = pieces.shape[0] // per
    rows = dot(spread_rows(per, count), pieces)
    return rows.reshape(per, 8, pieces.shape[1]).astype(BF)


def from_chunks(chunks, count):
    per, _, n = chunks.shape
    rows = chunks.astype(F32).reshape(per * 8, n).astype(BF)
    return dot_t0(spread_rows(per, count), rows).astype(BF)


def fold(rows, per):
    parts = []
    for s in range(rows.shape[0] // per):
        for b in range(rows.shape[1] // 128):
            parts.append(rows[s * per : (s + 1) * per, b * 128 : (b + 1) * 128])
    return jnp.concatenate(parts, axis=0)


def unfold(rows, per):
    return jnp.concatenate([rows[b * per : (b + 1) * per] for b in range(4)], axis=1)


def per_chunk(sums, chunks):
    n = sums.shape[1]
    take = lax.broadcasted_iota(jnp.int32, (128, 16), 0) >> 3
    take = jnp.where(take == lax.broadcasted_iota(jnp.int32, (128, 16), 1), 1.0, 0.0)
    lane = lax.broadcasted_iota(jnp.int32, (128, n), 0)
    col = lax.broadcasted_iota(jnp.int32, (128, n), 1)
    spaced = dot(take.astype(BF), sums.astype(BF))
    spaced = jnp.where((lane & 7) == (col & 7), spaced, 0.0).astype(BF)
    home = lax.broadcasted_iota(jnp.int32, (chunks, n), 1) >> 3
    home = jnp.where(home == lax.broadcasted_iota(jnp.int32, (chunks, n), 0), 1.0, 0.0)
    return dot_t1(home.astype(BF), spaced)


def act(value):
    sig = 0.5 * jnp.tanh(0.5 * value) + 0.5
    out = value * sig
    return out.astype(BF), sig + out * (1.0 - sig)


def norm_rows(value):
    centred = value - jnp.mean(value, axis=-1, keepdims=True)
    inv = lax.rsqrt(jnp.mean(centred * centred, axis=-1, keepdims=True) + EPS)
    return centred * inv, inv


def norm_back(grad, gain, normed, inv):
    scaled = grad * gain
    return inv * (
        scaled
        - jnp.mean(scaled, axis=-1, keepdims=True)
        - normed * jnp.mean(scaled * normed, axis=-1, keepdims=True)
    )


def col_sum(value):
    return jnp.sum(value, axis=0, keepdims=True)


def pre_kernel(
    core, idx, eb, eg, nb, ng, own_all, rec_all, cot_all, out, vec, ownb, recv, cotb, sems
):
    c = core[0]
    cp = [
        pltpu.make_async_copy(own_all.at[0, c], ownb, sems.at[0]),
        pltpu.make_async_copy(cot_all.at[c], cotb, sems.at[1]),
        pltpu.make_async_copy(rec_all.at[0, c], recv, sems.at[2]),
    ]
    for one in cp:
        one.start()
    vec[0:4, :] = eb[0]
    vec[4:5, :] = eg[...]
    vec[5:9, :] = nb[0]
    vec[9:10, :] = ng[...]
    vec[10:16, :] = jnp.zeros((6, vec.shape[1]), F32)
    rows = ownb.shape[0]
    h0, h1, hg = (hot_rows(idx[k : k + 1, :], rows).astype(BF) for k in range(3))
    for one in cp:
        one.wait()
    own, other = ownb[...], recv[...]
    low = jnp.where(c == 0, own.astype(F32), other.astype(F32)).astype(BF)
    top = jnp.where(c == 0, other.astype(F32), own.astype(F32)).astype(BF)
    pairs = ((h0, low), (h1, low), (h0, top), (h1, top), (hg, cotb[...]))
    pieces = jnp.concatenate([dot_t0(hot, src).astype(BF) for hot, src in pairs], axis=0)
    out[...] = to_chunks(pieces, idx.shape[1])


def post_kernel(idx, local, came, node_out, hang_out):
    rows = local.shape[0]
    per = came.shape[0]
    total = local[...]
    back = from_chunks(came[...], 8)
    for s in range(2):
        part = unfold(back[s * 4 * per : (s + 1) * 4 * per], per)
        total = total + dot(hot_rows(idx[s : s + 1, :], rows).astype(BF), part)
    low = total.astype(BF)
    node_out[...] = low
    hang = dot_t0(hot_rows(idx[2:3, :], rows).astype(BF), low).astype(BF)
    hang_out[...] = to_chunks(fold(hang, per), per)


def sum_kernel(idx, local, came, part_out, ship):
    per = came.shape[0]
    half = came.shape[2]
    part = jnp.sum(came[...].astype(F32), axis=0)
    part_out[...] = part
    tail = came[:, 72:80, :].astype(F32).reshape(per * 8, half).astype(BF)
    quarters = dot_t0(spread_rows(per, 5), tail).astype(BF)
    rows = local.shape[0]
    total = local[...]
    for s in range(2):
        back = jnp.concatenate(
            [quarters[(s + 2 * k) * per : (s + 2 * k + 1) * per, :] for k in range(2)], axis=1
        )
        total = total + dot(hot_rows(idx[s : s + 1, :], rows).astype(BF), back)
    ship[0:rows, :] = total.astype(BF)
    split_part(part, ship, rows)


def split_part(part, ship, rows):
    high = part.astype(BF)
    low = (part - high.astype(F32)).astype(BF)
    ship[rows:, :] = jnp.concatenate([high, low], axis=1)


def first_kernel(came, node, part_out, ship):
    rows = node.shape[0]
    part = jnp.sum(came[...].astype(F32), axis=0)
    part = jnp.concatenate([part, jnp.zeros((8, part.shape[1]), F32)], axis=0)
    part_out[...] = part
    ship[0:rows, :] = node[...]
    split_part(part, ship, rows)


def end_kernel(core, p0, p1, s0, s1, r0, r1, node_out, we, wem, wn, wnm):
    def part_of(ship):
        rows = node_out.shape[2]
        half = p0.shape[1]
        return ship[rows:, :half].astype(F32) + ship[rows:, half:].astype(F32)

    def write(left, right, first, second):
        full = jnp.concatenate([left, right], axis=1)
        rows = node_out.shape[2]
        node_out[0, 0] = first[0:rows, :]
        node_out[0, 1] = second[0:rows, :]
        we[0] = full[0:24, :]
        wem[0, 0] = full[24:32, :]
        wem[0, 1] = full[64:72, :]
        wn[0] = full[32:48, :]
        wnm[0, 0] = full[48:56, :]
        wnm[0, 1] = full[56:64, :]

    @pl.when(core[0] == 0)
    def _():
        write(p0[...], part_of(r0), s0, r0)

    @pl.when(core[0] == 1)
    def _():
        write(part_of(r1), p1[...], r1, s1)


SAVED = 14


def unit_kernel(mode, *refs):
    take = iter(refs)

    def some(n):
        return [next(take) for _ in range(n)]

    forward_part, backward_part = "F" in mode, "B" in mode
    scal, idx, erow, got = some(4)
    per = idx.shape[1]
    hang_in = next(take) if mode == "B" else None
    own_nodes, own_edges, *own_rest = some(7)
    recs = some(7)
    gout_all, gedge_all = some(2) if backward_part else (None, None)
    kept_in = some(SAVED) if mode == "B" else None
    bias_in = next(take) if mode == "B" else None
    saved_out = some(SAVED) if mode == "F" else None
    if backward_part:
        local_ref, edge_out, keep_out, send_out = some(4)
        back_ref, bias_ref, inc_out = some(3) if mode == "FB" else (None, None, None)
    dsts = some(7)
    nodes, edges, w1, wm, n1, nm, vec = dsts
    saved = some(SAVED)
    oh, a1, a2, s1, s2, nrm, inv, _, _, _, _, _, _, _ = saved
    q, msg, gout, gedge, l1, l2, l3, gag, bsum, inc = some(10)
    if backward_part:
        edge_ref, left_ref, right_ref = some(3)
    sems = next(take)
    sent = []

    def leave(src, dst, sem):
        pltpu.make_async_copy(src, dst, sems.at[sem]).start()

    is_own, c, node_count, edge_count, gi = (scal[i] for i in range(5))
    owns = [own_nodes.at[0, c], own_edges.at[0, c]] + [r.at[0] for r in own_rest[:4]]
    owns = owns + [own_rest[4]]
    recs = [recs[0].at[0, c], recs[1].at[0, c]] + recs[2:]
    if backward_part:
        cg = pltpu.make_async_copy(gout_all.at[gi], gout, sems.at[7])
        ce = pltpu.make_async_copy(gedge_all.at[gi], gedge, sems.at[8])
    loads = []
    if mode == "B":
        loads = [
            pltpu.make_async_copy(kept_in[k], saved[k], sems.at[9 + k]) for k in range(SAVED)
        ]

    def fetch(order):
        @pl.when(is_own == 1)
        def _():
            for k in order:
                pltpu.make_async_copy(owns[k], dsts[k], sems.at[k]).start()

        @pl.when(is_own == 0)
        def _():
            for k in order:
                pltpu.make_async_copy(recs[k], dsts[k], sems.at[k]).start()

    if mode == "B":
        cg.start()
        for k in range(7, SAVED):
            loads[k].start()
        fetch([6, 0, 5, 4])
    else:
        fetch([6, 0, 2, 1, 3])

    def ready(k):
        pltpu.make_async_copy(recs[k], dsts[k], sems.at[k]).wait()

    n_rows = nodes.shape[0]
    e_rows = edges.shape[0]
    width = nodes.shape[1]
    block = e_rows // (2 if mode == "F" else 1)
    blocks = e_rows // block

    def live_of(start, size, count):
        return (lax.broadcasted_iota(jnp.int32, (size, 1), 0) + start < count).astype(F32)

    ready(6)
    eb = [vec[i : i + 1, :] for i in range(4)]
    eg = vec[4:5, :]
    nb = [vec[i : i + 1, :] for i in range(5, 9)]
    ng = vec[9:10, :]
    to_target = hot_rows(erow[1:2, :], n_rows).astype(BF)

    if mode == "FB":
        pieces = from_chunks(got[...], 5)
        inc_out[...] = pieces[0 : 2 * per]
        inc[...] = pieces[2 * per : 4 * per]
        from_hanging = pieces[4 * per :]
    else:
        inc[...] = got[...]
        if backward_part:
            from_hanging = unfold(from_chunks(hang_in[...], 4), per)

    if forward_part:
        ecol = jnp.transpose(erow[...])
        grid = lax.broadcasted_iota(jnp.int32, (e_rows, width), 1)
        hit = (grid == ecol[:, 0:1]) | (grid == ecol[:, 1:2])
        oh[...] = jnp.where(hit, 1.0, 0.0).astype(BF)
        ready(0)
        ready(2)
        q[0:n_rows, :] = dot(nodes[...], w1[width : 2 * width, :]).astype(BF)
        q[n_rows : 2 * n_rows, :] = dot(nodes[...], w1[0:width, :]).astype(BF)
        q[2 * n_rows :, :] = dot(inc[...], w1[0:width, :]).astype(BF)
        ready(1)
        ready(3)
        fetch([4, 5])
        if backward_part:
            cg.start()
            ce.start()

        def forward(i, _):
            start = pl.multiple_of(i * block, block)
            rows = pl.ds(start, block)
            z = dot(oh[rows, :], q[...]) + dot(edges[rows, :], w1[2 * width :, :]) + eb[0]
            low, slope = act(z)
            a1[rows, :] = low
            s1[rows, :] = slope
            low, slope = act(dot(low, wm[0]) + eb[1])
            a2[rows, :] = low
            s2[rows, :] = slope
            normed, rstd = norm_rows(dot(low, wm[1]) + eb[2])
            nrm[rows, :] = normed
            inv[rows, :] = jnp.broadcast_to(rstd, (block, 128))
            msg[rows, :] = ((normed * eg + eb[3]) * live_of(start, block, edge_count)).astype(BF)
            if mode == "F":
                for k in range(7):
                    leave(saved[k].at[rows, :], saved_out[k].at[rows, :], 9 + k)
            return 0

        lax.fori_loop(0, blocks, forward, 0)

        agg = dot(to_target, msg[...]).astype(BF)
        ready(4)
        ready(5)
        x_n = nodes[...]
        na1, ns1 = act(dot(x_n, n1[0:width, :]) + dot(agg, n1[width:, :]) + nb[0])
        na2, ns2 = act(dot(na1, nm[0]) + nb[1])
        nn, nr = norm_rows(dot(na2, nm[1]) + nb[2])
        nr = jnp.broadcast_to(nr, (n_rows, 128))
        for ref, value in zip(saved[7:], (agg, na1, na2, ns1, ns2, nn, nr)):
            ref[...] = value

    if not backward_part:
        for k in range(7, SAVED):
            leave(saved[k], saved_out[k], 9 + k)
        for k in range(SAVED):
            pltpu.make_async_copy(saved[k], saved_out[k], sems.at[9 + k]).wait()
        return
    if not forward_part:
        ready(0)
        ready(4)
        ready(5)
        for one in loads[7:]:
            one.wait()
        for one in loads[:7]:
            one.start()
        fetch([3, 2, 1])
        ce.start()
    x_n = nodes[...]
    agg, na1, na2, ns1, ns2, nn, nr = (ref[...] for ref in saved[7:])

    def put(first, pieces):
        half = width // 2
        tile = jnp.concatenate([x.reshape(64, -1, x.shape[-1]) for x in pieces], axis=1)
        n = tile.shape[1]
        left_ref[:, first : first + n, :] = tile[:, :, :half].astype(BF)
        right_ref[:, first : first + n, :] = tile[:, :, half:].astype(BF)
        part = (slice(None), pl.ds(first, n), slice(None))

        def copies(one, two):
            return [
                pltpu.make_async_copy(ref.at[part], out.at[part], sems.at[24 + len(sent) * 2 + k])
                for k, (ref, out) in enumerate(((two, send_out), (one, keep_out)))
            ]

        @pl.when(c == 0)
        def _():
            for copy in copies(left_ref, right_ref):
                copy.start()

        @pl.when(c == 1)
        def _():
            for copy in copies(right_ref, left_ref):
                copy.start()

        sent.append(copies(left_ref, right_ref))

    cg.wait()
    hung = jnp.max(
        jnp.where(
            lax.broadcasted_iota(jnp.int32, (n_rows, idx.shape[1]), 0) == idx[2:3, :], 1.0, 0.0
        ),
        axis=1,
        keepdims=True,
    )
    spread = 0.5 * (hot_rows(idx[3:4, :], n_rows) + hot_rows(idx[4:5, :], n_rows))
    grad_new = gout[...].astype(F32) * (1.0 - hung) + dot(spread.astype(BF), from_hanging)
    gy = grad_new * live_of(0, n_rows, node_count)
    bsum[8:9, :] = col_sum(gy)
    bsum[9:10, :] = col_sum(gy * nn)
    g3 = norm_back(gy, ng, nn, nr[:, 0:1])
    bsum[7:8, :] = col_sum(g3)
    low3 = g3.astype(BF)
    g2 = dot_t1(low3, nm[1]) * ns2
    bsum[6:7, :] = col_sum(g2)
    low2 = g2.astype(BF)
    g1 = dot_t1(low2, nm[0]) * ns1
    bsum[5:6, :] = col_sum(g1)
    low1 = g1.astype(BF)
    direct = grad_new + dot_t1(low1, n1[0:width, :])
    gag[0:n_rows, :] = dot_t1(low1, n1[width:, :]).astype(BF)
    gag[n_rows:, :] = jnp.zeros((gag.shape[0] - n_rows, width), BF)
    put(32, [jnp.concatenate([dot_t0(x_n, low1), dot_t0(agg, low1)], axis=0)])
    put(48, [dot_t0(na1, low2), dot_t0(na2, low3)])

    if not forward_part:
        ready(1)
        ready(2)
        ready(3)
        for one in loads[:7]:
            one.wait()
    ce.wait()
    gk = gag.shape[0]

    def backward(i, carry):
        start = pl.multiple_of(i * block, block)
        rows = pl.ds(start, block)
        c1, c2, c3, c4, c5 = carry
        ge = gedge[rows, :].astype(F32)
        gy = (dot(oh[rows, 0:gk], gag[...]) + ge) * live_of(start, block, edge_count)
        normed = nrm[rows, :]
        g3 = norm_back(gy, eg, normed, inv[rows, 0:1])
        low = g3.astype(BF)
        l3[rows, :] = low
        g2 = dot_t1(low, wm[1]) * s2[rows, :]
        low = g2.astype(BF)
        l2[rows, :] = low
        g1 = dot_t1(low, wm[0]) * s1[rows, :]
        low = g1.astype(BF)
        l1[rows, :] = low
        edge_ref[rows, :] = (ge + dot_t1(low, w1[2 * width :, :])).astype(BF)
        leave(edge_ref.at[rows, :], edge_out.at[rows, :], 23)
        return (
            c1 + col_sum(g1),
            c2 + col_sum(g2),
            c3 + col_sum(g3),
            c4 + col_sum(gy),
            c5 + col_sum(gy * normed),
        )

    zero = jnp.zeros((1, width), F32)
    sums = lax.fori_loop(0, blocks, backward, (zero,) * 5)
    for k in range(5):
        bsum[k : k + 1, :] = sums[k]
    bsum[10:16, :] = jnp.zeros((6, width), F32)

    lowv = l1[...]
    t_sum = dot(to_target, lowv).astype(BF)
    from_source = hot_rows(erow[0:1, :] - n_rows, width - n_rows).astype(BF)
    s_sum = dot(from_source, lowv).astype(BF)
    d_ext = dot_t1(s_sum, w1[0:width, :])
    local_ref[...] = direct + d_ext[0:n_rows, :] + dot_t1(t_sum, w1[width : 2 * width, :])
    d_inc = d_ext[n_rows:, :].astype(BF)
    bias_row = per_chunk(bsum[...], per)
    half = width // 2
    extra = []
    if mode == "FB":
        back_ref[...] = to_chunks(fold(d_inc, per), per)
        bias_ref[...] = bias_row
    else:
        bias_row = jnp.concatenate([bias_row, bias_in[...]], axis=1).astype(BF)
        kept = jnp.concatenate([d_inc[:, :half], d_inc[:, half:], bias_row], axis=0)
        given = jnp.concatenate([jnp.zeros((4 * per, half), BF), bias_row], axis=0)
        one = jnp.where(c == 0, kept.astype(F32), given.astype(F32)).astype(BF)
        two = jnp.where(c == 0, given.astype(F32), kept.astype(F32)).astype(BF)
        place = spread_rows(per, 5)
        extra = [jnp.concatenate([dot(place, one), dot(place, two)], axis=1)]
    put(64, [dot_t0(a2[...], l3[...])] + extra)
    grad_w1 = jnp.concatenate(
        [
            dot_t0(x_n, s_sum[0:n_rows, :]) + dot_t0(inc[...], s_sum[n_rows:, :]),
            dot_t0(x_n, t_sum),
            dot_t0(edges[...], lowv),
        ],
        axis=0,
    )
    put(0, [grad_w1, dot_t0(a1[...], l2[...])])
    for pair in sent:
        for copy in pair:
            copy.wait()
    pltpu.make_async_copy(edge_ref, edge_out, sems.at[23]).wait()


VM = pl.BlockSpec(memory_space=pltpu.VMEM)
SM = pl.BlockSpec(memory_space=pltpu.SMEM)
HB = pl.BlockSpec(memory_space=pl.ANY)


def swap(x):
    return lax.ppermute(x, "pipe", [(0, 1), (1, 0)])


def exchange(x):
    return lax.all_to_all(x, "dom", split_axis=0, concat_axis=0, tiled=True)


def body(
    node_in, edge_in, cot_node, cot_edge, node_count, edge_count, edge_source, edge_target,
    halo_send, hang_send, parent_rows,
    w_edge_in, w_edge_mid, edge_bias, edge_gain, w_node_in, w_node_mid, node_bias, node_gain,
):
    n_rows, width = node_in.shape[2:]
    e_rows = edge_in.shape[2]
    peers = lax.axis_size("dom")
    slots = halo_send.shape[2]
    c = lax.axis_index("pipe")
    half = width // 2

    rec_nodes = swap(node_in)

    hs, gs, ps = halo_send[0], hang_send[0], parent_rows[0]
    idx = jnp.stack([hs[:, 0], hs[:, 1], gs[:, 0], ps[:, 0], ps[:, 1]] + [hs[:, 0]] * 3)
    rec_nodes, idx = lax.optimization_barrier((rec_nodes, idx))
    outs, vec = pl.pallas_call(
        pre_kernel,
        out_shape=[
            jax.ShapeDtypeStruct((peers, 8, width), BF),
            jax.ShapeDtypeStruct((16, width), F32),
        ],
        in_specs=[SM] + [VM] * 5 + [HB] * 3,
        out_specs=[VM] * 2,
        scratch_shapes=[pltpu.VMEM((n_rows, width), BF)] * 3 + [pltpu.SemaphoreType.DMA((3,))],
        name="pre",
    )(
        c.reshape(1), idx, edge_bias, edge_gain, node_bias, node_gain,
        node_in, rec_nodes, cot_node,
    )
    rec_vec = swap(vec)
    bulk = (edge_in, w_edge_in, w_edge_mid, w_node_in, w_node_mid)
    bulk, _ = lax.optimization_barrier((bulk, rec_nodes))
    rec_edges = swap(bulk[0])
    rec_w1, rec_wm, rec_n1, rec_nm = (swap(w[0]) for w in bulk[1:])
    bulk = (rec_edges, rec_w1, rec_wm, rec_n1, rec_nm, edge_source, edge_target)
    bulk = lax.optimization_barrier(bulk)
    rec_edges, rec_w1, rec_wm, rec_n1, rec_nm, edge_source, edge_target = bulk
    k = edge_source - n_rows
    source = jnp.where(k < 0, edge_source, n_rows + (k % slots) * peers + k // slots)
    erow = jnp.stack([n_rows + source, edge_target] + [edge_target] * 6, axis=0)

    got = exchange(outs)

    shape = jax.ShapeDtypeStruct
    saved = [shape((e_rows, width), BF)] * 3 + [shape((e_rows, width), F32)] * 3
    saved += [shape((e_rows, 128), F32)]
    saved += [shape((n_rows, width), BF)] * 3 + [shape((n_rows, width), F32)] * 3
    saved += [shape((n_rows, 128), F32)]

    def results(mode):
        chunk = shape((peers, 72 if mode == "FB" else 80, half), BF)
        some = [shape((n_rows, width), F32), shape((e_rows, width), BF), chunk, chunk]
        if mode == "FB":
            some += [shape((peers, 8, 128), BF), shape((peers, 128), F32)]
            some += [shape((slots * peers, width), BF)]
        return some

    stages = [
        shape((n_rows, width), BF),
        shape((e_rows, width), BF),
        shape(w_edge_in.shape[1:], BF),
        shape(w_edge_mid.shape[1:], BF),
        shape(w_node_in.shape[1:], BF),
        shape(w_node_mid.shape[1:], BF),
        shape((16, width), F32),
    ]
    work = [
        shape((width, width), BF),
        shape((e_rows, width), BF),
        shape((n_rows, width), BF),
        shape((e_rows, width), BF),
        shape((e_rows, width), BF),
        shape((e_rows, width), BF),
        shape((e_rows, width), BF),
        shape((256, width), BF),
        shape((16, width), F32),
        shape((slots * peers, width), BF),
    ]

    def run(mode, layer, got, hang_l=None, gout=None, gedge=None, gi=0, kept=(), bias=()):
        own = (c == layer).astype(jnp.int32)
        scal = jnp.stack([own, c, node_count[0], edge_count[0], jnp.int32(gi)]).astype(jnp.int32)
        back = "B" in mode
        arrays = [scal, idx, erow, got] + ([hang_l] if mode == "B" else [])
        near = len(arrays) - 1
        arrays += [node_in, edge_in, w_edge_in, w_edge_mid, w_node_in, w_node_mid, vec]
        arrays += [rec_nodes, rec_edges, rec_w1, rec_wm, rec_n1, rec_nm, rec_vec]
        arrays += ([gout, gedge] if back else []) + list(kept)
        far = len(arrays)
        arrays += list(bias)
        outs = (saved if mode == "F" else []) + (results(mode) if back else [])
        scratch = stages + saved + work + (results(mode)[1:4] if back else [])
        out_specs = [HB] * len(outs)
        if back:
            out_specs = [VM, HB, HB, HB] + [VM] * (len(outs) - 4)
        return pl.pallas_call(
            functools.partial(unit_kernel, mode),
            out_shape=outs,
            in_specs=[SM] + [VM] * near + [HB] * (far - near - 1) + [VM] * len(bias),
            out_specs=out_specs,
            scratch_shapes=[pltpu.VMEM(x.shape, x.dtype) for x in scratch]
            + [pltpu.SemaphoreType.DMA((40,))],
            compiler_params=pltpu.CompilerParams(vmem_limit_bytes=56 * 1024 * 1024),
        )(*arrays)

    post = pl.pallas_call(
        post_kernel,
        out_shape=[shape((n_rows, width), BF), shape((peers, 8, 128), BF)],
        in_specs=[VM] * 3,
        out_specs=[VM] * 2,
        name="post",
    )

    def paired(keep, send):
        return (keep.astype(F32) + swap(send).astype(F32)).astype(BF)

    local1, edge1, keep1, send1, back1, bias1, inc0 = run("FB", 1, got, None, cot_node, cot_edge, c)
    kept0 = run("F", 0, inc0)
    node1, hang1 = post(idx, local1, exchange(back1))
    hang_in0 = exchange(hang1)
    mine1, hang_in0 = lax.optimization_barrier((paired(keep1, send1), hang_in0))
    came1 = exchange(mine1)
    local0, edge0, keep0, send0 = run(
        "B", 0, inc0, hang_in0, node1[None], edge1[None], 0, kept0, [bias1]
    )
    up = [(0, 1)]
    down = [(1, 0)]
    first = c == 0
    came0 = exchange(paired(keep0, send0))
    sums_out = [shape((80, half), F32), shape((n_rows + 80, width), BF)]
    part1, ship1 = pl.pallas_call(
        first_kernel,
        out_shape=sums_out,
        in_specs=[VM] * 2,
        out_specs=[VM] * 2,
        name="sums1",
    )(came1, node1)
    part0, ship0 = pl.pallas_call(
        sum_kernel,
        out_shape=sums_out,
        in_specs=[VM] * 3,
        out_specs=[VM] * 2,
        name="sums0",
    )(idx, local0, came0)
    lower = lax.ppermute(edge0, "pipe", down)
    upper = lax.ppermute(edge1, "pipe", up)
    edge_final = jnp.where(first, jnp.stack([edge0, lower]), jnp.stack([upper, edge1]))[None]
    r0 = lax.ppermute(ship0, "pipe", down)
    r1 = lax.ppermute(ship1, "pipe", up)
    node_final, we, wem, wn, wnm = pl.pallas_call(
        end_kernel,
        out_shape=[
            shape((1, 2, n_rows, width), BF),
            shape((1, 24, width), F32),
            shape((1, 2, 8, width), F32),
            shape((1, 16, width), F32),
            shape((1, 2, 8, width), F32),
        ],
        in_specs=[SM] + [VM] * 6,
        out_specs=[VM] * 5,
        name="end",
    )(c.reshape(1), part0, part1, ship0, ship1, r0, r1)
    bias = jnp.where(first, part0[76, 0:128], part0[76, 128:256]).reshape(16, 8)
    return (
        node_final,
        edge_final,
        we,
        wem,
        bias[None, 0:4],
        bias[4:5],
        wn,
        wnm,
        bias[None, 5:9],
        bias[9:10],
    )


def solution(mesh):
    dom3 = P("dom", None, None)
    in_specs = (
        P("pipe", None, "dom", None),
        P("pipe", None, "dom", None),
        P(None, "dom", None),
        P(None, "dom", None),
        P("dom"),
        P("dom"),
        P("dom"),
        P("dom"),
        dom3,
        dom3,
        dom3,
        P("pipe", None, None),
        P("pipe", None, None, None),
        P("pipe", None, None),
        P("pipe", None),
        P("pipe", None, None),
        P("pipe", None, None, None),
        P("pipe", None, None),
        P("pipe", None),
    )
    out_specs = (
        P("pipe", None, "dom", None),
        P("pipe", None, "dom", None),
        P("pipe", "dom", None),
        P("pipe", None, "dom", None),
        P("pipe", None, "dom"),
        P("pipe", "dom"),
        P("pipe", "dom", None),
        P("pipe", None, "dom", None),
        P("pipe", None, "dom"),
        P("pipe", "dom"),
    )
    return jax.shard_map(body, mesh=mesh, in_specs=in_specs, out_specs=out_specs, check_vma=False)
```

```python
import functools

import jax
import jax.numpy as jnp
from jax import lax
from jax.experimental import pallas as pl
from jax.experimental.pallas import tpu as pltpu
from jax.sharding import PartitionSpec as P

EPS = 1e-05
BF = jnp.bfloat16
F32 = jnp.float32


def dot(a, b):
    return lax.dot_general(a, b, (((1,), (0,)), ((), ())), preferred_element_type=F32)


def dot_t0(a, b):
    return lax.dot_general(a, b, (((0,), (0,)), ((), ())), preferred_element_type=F32)


def dot_t1(a, b):
    return lax.dot_general(a, b, (((1,), (1,)), ((), ())), preferred_element_type=F32)


def hot_rows(index_row, rows):
    grid = lax.broadcasted_iota(jnp.int32, (rows, index_row.shape[1]), 0)
    return jnp.where(grid == index_row, 1.0, 0.0)


def spread_rows(per, count):
    shape = (8 * per, count * per)
    row = lax.broadcasted_iota(jnp.int32, shape, 0)
    col = lax.broadcasted_iota(jnp.int32, shape, 1)
    return jnp.where(col == (row & 7) * per + (row >> 3), 1.0, 0.0).astype(BF)


def to_chunks(pieces, per):
    count = pieces.shape[0] // per
    rows = dot(spread_rows(per, count), pieces)
    return rows.reshape(per, 8, pieces.shape[1]).astype(BF)


def from_chunks(chunks, count):
    per, _, n = chunks.shape
    rows = chunks.astype(F32).reshape(per * 8, n).astype(BF)
    return dot_t0(spread_rows(per, count), rows).astype(BF)


def fold(rows, per):
    parts = []
    for s in range(rows.shape[0] // per):
        for b in range(rows.shape[1] // 128):
            parts.append(rows[s * per : (s + 1) * per, b * 128 : (b + 1) * 128])
    return jnp.concatenate(parts, axis=0)


def close_rows(pieces, per):
    rows = fold(pieces, per)
    rows = jnp.concatenate([rows, jnp.zeros((4 * per, 128), BF)], axis=0)
    step = 8 * per
    return jnp.concatenate(
        [to_chunks(rows[g * step : (g + 1) * step], per) for g in range(3)], axis=2
    )


def open_rows(chunks, count):
    per = chunks.shape[0]
    parts = [from_chunks(chunks[:, :, g * 128 : (g + 1) * 128], 8) for g in range(3)]
    rows = jnp.concatenate(parts, axis=0)
    step = 4 * per
    return jnp.concatenate(
        [unfold(rows[k * step : (k + 1) * step], per) for k in range(count)], axis=0
    )


def unfold(rows, per):
    return jnp.concatenate([rows[b * per : (b + 1) * per] for b in range(4)], axis=1)


def per_chunk(sums, chunks):
    n = sums.shape[1]
    take = lax.broadcasted_iota(jnp.int32, (128, 16), 0) >> 3
    take = jnp.where(take == lax.broadcasted_iota(jnp.int32, (128, 16), 1), 1.0, 0.0)
    lane = lax.broadcasted_iota(jnp.int32, (128, n), 0)
    col = lax.broadcasted_iota(jnp.int32, (128, n), 1)
    spaced = dot(take.astype(BF), sums.astype(BF))
    spaced = jnp.where((lane & 7) == (col & 7), spaced, 0.0).astype(BF)
    home = lax.broadcasted_iota(jnp.int32, (chunks, n), 1) >> 3
    home = jnp.where(home == lax.broadcasted_iota(jnp.int32, (chunks, n), 0), 1.0, 0.0)
    return dot_t1(home.astype(BF), spaced)


def act(value):
    sig = 0.5 * jnp.tanh(0.5 * value) + 0.5
    out = value * sig
    return out.astype(BF), sig + out * (1.0 - sig)


def norm_rows(value):
    centred = value - jnp.mean(value, axis=-1, keepdims=True)
    inv = lax.rsqrt(jnp.mean(centred * centred, axis=-1, keepdims=True) + EPS)
    return centred * inv, inv


def norm_back(grad, gain, normed, inv):
    scaled = grad * gain
    return inv * (
        scaled
        - jnp.mean(scaled, axis=-1, keepdims=True)
        - normed * jnp.mean(scaled * normed, axis=-1, keepdims=True)
    )


def col_sum(value):
    return jnp.sum(value, axis=0, keepdims=True)


def pre_kernel(
    core, idx, eb, eg, nb, ng, own_all, rec_all, cot_all, out, vec, ownb, recv, cotb, sems
):
    c = core[0]
    cp = [
        pltpu.make_async_copy(own_all.at[0, c], ownb, sems.at[0]),
        pltpu.make_async_copy(cot_all.at[c], cotb, sems.at[1]),
        pltpu.make_async_copy(rec_all.at[0, c], recv, sems.at[2]),
    ]
    for one in cp:
        one.start()
    vec[0:4, :] = eb[0]
    vec[4:5, :] = eg[...]
    vec[5:9, :] = nb[0]
    vec[9:10, :] = ng[...]
    vec[10:16, :] = jnp.zeros((6, vec.shape[1]), F32)
    rows = ownb.shape[0]
    h0, h1, hg = (hot_rows(idx[k : k + 1, :], rows).astype(BF) for k in range(3))
    for one in cp:
        one.wait()
    own, other = ownb[...], recv[...]
    low = jnp.where(c == 0, own.astype(F32), other.astype(F32)).astype(BF)
    top = jnp.where(c == 0, other.astype(F32), own.astype(F32)).astype(BF)
    pairs = ((h0, low), (h1, low), (h0, top), (h1, top), (hg, cotb[...]))
    pieces = jnp.concatenate([dot_t0(hot, src).astype(BF) for hot, src in pairs], axis=0)
    out[...] = close_rows(pieces, idx.shape[1])


def post_kernel(idx, local, came, node_out, hang_out):
    rows = local.shape[0]
    per = came.shape[0]
    total = local[...]
    back = from_chunks(came[...], 8)
    for s in range(2):
        part = unfold(back[s * 4 * per : (s + 1) * 4 * per], per)
        total = total + dot(hot_rows(idx[s : s + 1, :], rows).astype(BF), part)
    low = total.astype(BF)
    node_out[...] = low
    hang = dot_t0(hot_rows(idx[2:3, :], rows).astype(BF), low).astype(BF)
    hang_out[...] = to_chunks(fold(hang, per), per)


def sum_kernel(idx, local, came, part_out, ship):
    per = came.shape[0]
    half = came.shape[2]
    part = jnp.sum(came[...].astype(F32), axis=0)
    part_out[...] = part
    tail = came[:, 72:80, :].astype(F32).reshape(per * 8, half).astype(BF)
    quarters = dot_t0(spread_rows(per, 5), tail).astype(BF)
    rows = local.shape[0]
    total = local[...]
    for s in range(2):
        back = jnp.concatenate(
            [quarters[(s + 2 * k) * per : (s + 2 * k + 1) * per, :] for k in range(2)], axis=1
        )
        total = total + dot(hot_rows(idx[s : s + 1, :], rows).astype(BF), back)
    ship[0:rows, :] = total.astype(BF)
    split_part(part, ship, rows)


def split_part(part, ship, rows):
    high = part.astype(BF)
    low = (part - high.astype(F32)).astype(BF)
    ship[rows:, :] = jnp.concatenate([high, low], axis=1)


def first_kernel(came, node, part_out, ship):
    rows = node.shape[0]
    part = jnp.sum(came[...].astype(F32), axis=0)
    part = jnp.concatenate([part, jnp.zeros((8, part.shape[1]), F32)], axis=0)
    part_out[...] = part
    ship[0:rows, :] = node[...]
    split_part(part, ship, rows)


def end_kernel(core, p0, p1, s0, s1, r0, r1, node_out, we, wem, wn, wnm):
    def part_of(ship):
        rows = node_out.shape[2]
        half = p0.shape[1]
        return ship[rows:, :half].astype(F32) + ship[rows:, half:].astype(F32)

    def write(left, right, first, second):
        full = jnp.concatenate([left, right], axis=1)
        rows = node_out.shape[2]
        node_out[0, 0] = first[0:rows, :]
        node_out[0, 1] = second[0:rows, :]
        we[0] = full[0:24, :]
        wem[0, 0] = full[24:32, :]
        wem[0, 1] = full[64:72, :]
        wn[0] = full[32:48, :]
        wnm[0, 0] = full[48:56, :]
        wnm[0, 1] = full[56:64, :]

    @pl.when(core[0] == 0)
    def _():
        write(p0[...], part_of(r0), s0, r0)

    @pl.when(core[0] == 1)
    def _():
        write(part_of(r1), p1[...], r1, s1)


SAVED = 7


def unit_kernel(mode, *refs):
    take = iter(refs)

    def some(n):
        return [next(take) for _ in range(n)]

    scal, idx, erow, got = some(4)
    per = idx.shape[1]
    hang_in = next(take) if mode == 0 else None
    own_nodes, own_edges, *own_rest = some(7)
    recs = some(7)
    gout_all, gedge_all = some(2)
    bias_in = next(take) if mode == 0 else None
    local_ref, edge_out, keep_out, send_out = some(4)
    back_ref, bias_ref, inc_out = some(3) if mode == 1 else (None, None, None)
    dsts = some(7)
    nodes, edges, w1, wm, n1, nm, vec = dsts
    saved = some(SAVED)
    oh, a1, a2, s1, s2, nrm, inv = saved
    q, msg, gout, gedge, l1, l2, l3, gag, bsum, inc = some(10)
    edge_ref, left_ref, right_ref = some(3)
    sems = next(take)
    sent = []


    is_own, c, node_count, edge_count, gi = (scal[i] for i in range(5))
    owns = [own_nodes.at[0, c], own_edges.at[0, c]] + [r.at[0] for r in own_rest[:4]]
    owns = owns + [own_rest[4]]
    recs = [recs[0].at[0, c], recs[1].at[0, c]] + recs[2:]
    cg = pltpu.make_async_copy(gout_all.at[gi], gout, sems.at[7])
    ce = pltpu.make_async_copy(gedge_all.at[gi], gedge, sems.at[8])

    def fetch(order):
        @pl.when(is_own == 1)
        def _():
            for k in order:
                pltpu.make_async_copy(owns[k], dsts[k], sems.at[k]).start()

        @pl.when(is_own == 0)
        def _():
            for k in order:
                pltpu.make_async_copy(recs[k], dsts[k], sems.at[k]).start()

    fetch([6, 0, 2, 1, 3])

    def ready(k):
        pltpu.make_async_copy(recs[k], dsts[k], sems.at[k]).wait()

    n_rows = nodes.shape[0]
    e_rows = edges.shape[0]
    width = nodes.shape[1]
    block = e_rows
    blocks = e_rows // block

    def live_of(start, size, count):
        return (lax.broadcasted_iota(jnp.int32, (size, 1), 0) + start < count).astype(F32)

    ready(6)
    eb = [vec[i : i + 1, :] for i in range(4)]
    eg = vec[4:5, :]
    nb = [vec[i : i + 1, :] for i in range(5, 9)]
    ng = vec[9:10, :]
    to_target = hot_rows(erow[1:2, :], n_rows).astype(BF)

    if mode == 1:
        pieces = open_rows(got[...], 5)
        inc_out[...] = pieces[0 : 2 * per]
        inc[...] = pieces[2 * per : 4 * per]
        from_hanging = pieces[4 * per :]
    else:
        inc[...] = got[...]
        from_hanging = unfold(from_chunks(hang_in[...], 4), per)

    ecol = jnp.transpose(erow[...])
    grid = lax.broadcasted_iota(jnp.int32, (e_rows, width), 1)
    hit = (grid == ecol[:, 0:1]) | (grid == ecol[:, 1:2])
    oh[...] = jnp.where(hit, 1.0, 0.0).astype(BF)
    ready(0)
    ready(2)
    q[0:n_rows, :] = dot(nodes[...], w1[width : 2 * width, :]).astype(BF)
    q[n_rows : 2 * n_rows, :] = dot(nodes[...], w1[0:width, :]).astype(BF)
    q[2 * n_rows :, :] = dot(inc[...], w1[0:width, :]).astype(BF)
    ready(1)
    ready(3)
    fetch([4, 5])
    cg.start()
    ce.start()

    def forward(i, _):
        start = pl.multiple_of(i * block, block)
        rows = pl.ds(start, block)
        z = dot(oh[rows, :], q[...]) + dot(edges[rows, :], w1[2 * width :, :]) + eb[0]
        low, slope = act(z)
        a1[rows, :] = low
        s1[rows, :] = slope
        low, slope = act(dot(low, wm[0]) + eb[1])
        a2[rows, :] = low
        s2[rows, :] = slope
        normed, rstd = norm_rows(dot(low, wm[1]) + eb[2])
        nrm[rows, :] = normed
        inv[rows, :] = jnp.broadcast_to(rstd, (block, 128))
        msg[rows, :] = ((normed * eg + eb[3]) * live_of(start, block, edge_count)).astype(BF)
        return 0

    lax.fori_loop(0, blocks, forward, 0)

    agg = dot(to_target, msg[...]).astype(BF)
    ready(4)
    ready(5)
    x_n = nodes[...]
    na1, ns1 = act(dot(x_n, n1[0:width, :]) + dot(agg, n1[width:, :]) + nb[0])
    na2, ns2 = act(dot(na1, nm[0]) + nb[1])
    nn, nr = norm_rows(dot(na2, nm[1]) + nb[2])
    nr = jnp.broadcast_to(nr, (n_rows, 128))


    def put(first, pieces):
        half = width // 2
        tile = jnp.concatenate([x.reshape(64, -1, x.shape[-1]) for x in pieces], axis=1)
        n = tile.shape[1]
        left_ref[:, first : first + n, :] = tile[:, :, :half].astype(BF)
        right_ref[:, first : first + n, :] = tile[:, :, half:].astype(BF)
        part = (slice(None), pl.ds(first, n), slice(None))

        def copies(one, two):
            return [
                pltpu.make_async_copy(ref.at[part], out.at[part], sems.at[24 + len(sent) * 2 + k])
                for k, (ref, out) in enumerate(((two, send_out), (one, keep_out)))
            ]

        @pl.when(c == 0)
        def _():
            for copy in copies(left_ref, right_ref):
                copy.start()

        @pl.when(c == 1)
        def _():
            for copy in copies(right_ref, left_ref):
                copy.start()

        sent.append(copies(left_ref, right_ref))

    cg.wait()
    hung = jnp.max(
        jnp.where(
            lax.broadcasted_iota(jnp.int32, (n_rows, idx.shape[1]), 0) == idx[2:3, :], 1.0, 0.0
        ),
        axis=1,
        keepdims=True,
    )
    spread = 0.5 * (hot_rows(idx[3:4, :], n_rows) + hot_rows(idx[4:5, :], n_rows))
    grad_new = gout[...].astype(F32) * (1.0 - hung) + dot(spread.astype(BF), from_hanging)
    gy = grad_new * live_of(0, n_rows, node_count)
    bsum[8:9, :] = col_sum(gy)
    bsum[9:10, :] = col_sum(gy * nn)
    g3 = norm_back(gy, ng, nn, nr[:, 0:1])
    bsum[7:8, :] = col_sum(g3)
    low3 = g3.astype(BF)
    g2 = dot_t1(low3, nm[1]) * ns2
    bsum[6:7, :] = col_sum(g2)
    low2 = g2.astype(BF)
    g1 = dot_t1(low2, nm[0]) * ns1
    bsum[5:6, :] = col_sum(g1)
    low1 = g1.astype(BF)
    direct = grad_new + dot_t1(low1, n1[0:width, :])
    gag[0:n_rows, :] = dot_t1(low1, n1[width:, :]).astype(BF)
    gag[n_rows:, :] = jnp.zeros((gag.shape[0] - n_rows, width), BF)
    put(32, [jnp.concatenate([dot_t0(x_n, low1), dot_t0(agg, low1)], axis=0)])
    put(48, [dot_t0(na1, low2), dot_t0(na2, low3)])

    ce.wait()
    gk = gag.shape[0]

    def backward(i, carry):
        start = pl.multiple_of(i * block, block)
        rows = pl.ds(start, block)
        c1, c2, c3, c4, c5 = carry
        ge = gedge[rows, :].astype(F32)
        gy = (dot(oh[rows, 0:gk], gag[...]) + ge) * live_of(start, block, edge_count)
        normed = nrm[rows, :]
        g3 = norm_back(gy, eg, normed, inv[rows, 0:1])
        low = g3.astype(BF)
        l3[rows, :] = low
        g2 = dot_t1(low, wm[1]) * s2[rows, :]
        low = g2.astype(BF)
        l2[rows, :] = low
        g1 = dot_t1(low, wm[0]) * s1[rows, :]
        low = g1.astype(BF)
        l1[rows, :] = low
        edge_ref[rows, :] = (ge + dot_t1(low, w1[2 * width :, :])).astype(BF)
        pltpu.make_async_copy(edge_ref.at[rows, :], edge_out.at[rows, :], sems.at[23]).start()
        return (
            c1 + col_sum(g1),
            c2 + col_sum(g2),
            c3 + col_sum(g3),
            c4 + col_sum(gy),
            c5 + col_sum(gy * normed),
        )

    zero = jnp.zeros((1, width), F32)
    sums = lax.fori_loop(0, blocks, backward, (zero,) * 5)
    for k in range(5):
        bsum[k : k + 1, :] = sums[k]
    bsum[10:16, :] = jnp.zeros((6, width), F32)

    lowv = l1[...]
    t_sum = dot(to_target, lowv).astype(BF)
    from_source = hot_rows(erow[0:1, :] - n_rows, width - n_rows).astype(BF)
    s_sum = dot(from_source, lowv).astype(BF)
    d_ext = dot_t1(s_sum, w1[0:width, :])
    local_ref[...] = direct + d_ext[0:n_rows, :] + dot_t1(t_sum, w1[width : 2 * width, :])
    d_inc = d_ext[n_rows:, :].astype(BF)
    bias_row = per_chunk(bsum[...], per)
    half = width // 2
    extra = []
    if mode == 1:
        back_ref[...] = to_chunks(fold(d_inc, per), per)
        bias_ref[...] = bias_row
    else:
        bias_row = jnp.concatenate([bias_row, bias_in[...]], axis=1).astype(BF)
        kept = jnp.concatenate([d_inc[:, :half], d_inc[:, half:], bias_row], axis=0)
        given = jnp.concatenate([jnp.zeros((4 * per, half), BF), bias_row], axis=0)
        one = jnp.where(c == 0, kept.astype(F32), given.astype(F32)).astype(BF)
        two = jnp.where(c == 0, given.astype(F32), kept.astype(F32)).astype(BF)
        place = spread_rows(per, 5)
        extra = [jnp.concatenate([dot(place, one), dot(place, two)], axis=1)]
    put(64, [dot_t0(a2[...], l3[...])] + extra)
    grad_w1 = jnp.concatenate(
        [
            dot_t0(x_n, s_sum[0:n_rows, :]) + dot_t0(inc[...], s_sum[n_rows:, :]),
            dot_t0(x_n, t_sum),
            dot_t0(edges[...], lowv),
        ],
        axis=0,
    )
    put(0, [grad_w1, dot_t0(a1[...], l2[...])])
    for pair in sent:
        for copy in pair:
            copy.wait()
    pltpu.make_async_copy(edge_ref, edge_out, sems.at[23]).wait()


VM = pl.BlockSpec(memory_space=pltpu.VMEM)
SM = pl.BlockSpec(memory_space=pltpu.SMEM)
HB = pl.BlockSpec(memory_space=pl.ANY)


def swap(x):
    return lax.ppermute(x, "pipe", [(0, 1), (1, 0)])


def exchange(x):
    return lax.all_to_all(x, "dom", split_axis=0, concat_axis=0, tiled=True)


def body(
    node_in, edge_in, cot_node, cot_edge, node_count, edge_count, edge_source, edge_target,
    halo_send, hang_send, parent_rows,
    w_edge_in, w_edge_mid, edge_bias, edge_gain, w_node_in, w_node_mid, node_bias, node_gain,
):
    n_rows, width = node_in.shape[2:]
    e_rows = edge_in.shape[2]
    peers = lax.axis_size("dom")
    slots = halo_send.shape[2]
    c = lax.axis_index("pipe")
    half = width // 2

    rec_nodes = swap(node_in)

    hs, gs, ps = halo_send[0], hang_send[0], parent_rows[0]
    idx = jnp.stack([hs[:, 0], hs[:, 1], gs[:, 0], ps[:, 0], ps[:, 1]] + [hs[:, 0]] * 3)
    rec_nodes, idx = lax.optimization_barrier((rec_nodes, idx))
    outs, vec = pl.pallas_call(
        pre_kernel,
        out_shape=[
            jax.ShapeDtypeStruct((peers, 8, 384), BF),
            jax.ShapeDtypeStruct((16, width), F32),
        ],
        in_specs=[SM] + [VM] * 5 + [HB] * 3,
        out_specs=[VM] * 2,
        scratch_shapes=[pltpu.VMEM((n_rows, width), BF)] * 3 + [pltpu.SemaphoreType.DMA((3,))],
        name="pre",
    )(
        c.reshape(1), idx, edge_bias, edge_gain, node_bias, node_gain,
        node_in, rec_nodes, cot_node,
    )
    rec_vec = swap(vec)
    bulk = (edge_in, w_edge_in, w_edge_mid, w_node_in, w_node_mid)
    bulk, _ = lax.optimization_barrier((bulk, rec_nodes))
    rec_edges = swap(bulk[0])
    rec_w1, rec_wm, rec_n1, rec_nm = (swap(w[0]) for w in bulk[1:])
    bulk = (rec_edges, rec_w1, rec_wm, rec_n1, rec_nm, edge_source, edge_target)
    bulk = lax.optimization_barrier(bulk)
    rec_edges, rec_w1, rec_wm, rec_n1, rec_nm, edge_source, edge_target = bulk
    k = edge_source - n_rows
    source = jnp.where(k < 0, edge_source, n_rows + (k % slots) * peers + k // slots)
    erow = jnp.stack([n_rows + source, edge_target] + [edge_target] * 6, axis=0)

    got = exchange(outs)

    shape = jax.ShapeDtypeStruct
    saved = [shape((e_rows, width), BF)] * 3 + [shape((e_rows, width), F32)] * 3
    saved += [shape((e_rows, 128), F32)]

    def results(mode):
        chunk = shape((peers, 72 if mode == 1 else 80, half), BF)
        some = [shape((n_rows, width), F32), shape((e_rows, width), BF), chunk, chunk]
        if mode == 1:
            some += [shape((peers, 8, 128), BF), shape((peers, 128), F32)]
            some += [shape((slots * peers, width), BF)]
        return some

    stages = [
        shape((n_rows, width), BF),
        shape((e_rows, width), BF),
        shape(w_edge_in.shape[1:], BF),
        shape(w_edge_mid.shape[1:], BF),
        shape(w_node_in.shape[1:], BF),
        shape(w_node_mid.shape[1:], BF),
        shape((16, width), F32),
    ]
    work = [
        shape((width, width), BF),
        shape((e_rows, width), BF),
        shape((n_rows, width), BF),
        shape((e_rows, width), BF),
        shape((e_rows, width), BF),
        shape((e_rows, width), BF),
        shape((e_rows, width), BF),
        shape((256, width), BF),
        shape((16, width), F32),
        shape((slots * peers, width), BF),
    ]

    def run(layer, got, gout, gedge, gi, hang_l=(), bias=()):
        own = (c == layer).astype(jnp.int32)
        scal = jnp.stack([own, c, node_count[0], edge_count[0], jnp.int32(gi)]).astype(jnp.int32)
        arrays = [scal, idx, erow, got] + list(hang_l)
        near = len(arrays) - 1
        arrays += [node_in, edge_in, w_edge_in, w_edge_mid, w_node_in, w_node_mid, vec]
        arrays += [rec_nodes, rec_edges, rec_w1, rec_wm, rec_n1, rec_nm, rec_vec]
        arrays += [gout, gedge]
        far = len(arrays)
        arrays += list(bias)
        outs = results(layer)
        return pl.pallas_call(
            functools.partial(unit_kernel, layer),
            out_shape=outs,
            in_specs=[SM] + [VM] * near + [HB] * (far - near - 1) + [VM] * len(bias),
            out_specs=[VM, HB, HB, HB] + [VM] * (len(outs) - 4),
            scratch_shapes=[pltpu.VMEM(x.shape, x.dtype) for x in stages + saved + work + outs[1:4]]
            + [pltpu.SemaphoreType.DMA((40,))],
            compiler_params=pltpu.CompilerParams(vmem_limit_bytes=60 * 1024 * 1024),
        )(*arrays)

    post = pl.pallas_call(
        post_kernel,
        out_shape=[shape((n_rows, width), BF), shape((peers, 8, 128), BF)],
        in_specs=[VM] * 3,
        out_specs=[VM] * 2,
        name="post",
    )

    def paired(keep, send):
        return (keep.astype(F32) + swap(send).astype(F32)).astype(BF)

    local1, edge1, keep1, send1, back1, bias1, inc0 = run(1, got, cot_node, cot_edge, c)
    node1, hang1 = post(idx, local1, exchange(back1))
    hang_in0 = exchange(hang1)
    mine1, hang_in0 = lax.optimization_barrier((paired(keep1, send1), hang_in0))
    came1 = exchange(mine1)
    local0, edge0, keep0, send0 = run(
        0, inc0, node1[None], edge1[None], 0, [hang_in0], [bias1]
    )
    up = [(0, 1)]
    down = [(1, 0)]
    first = c == 0
    came0 = exchange(paired(keep0, send0))
    sums_out = [shape((80, half), F32), shape((n_rows + 80, width), BF)]
    part1, ship1 = pl.pallas_call(
        first_kernel,
        out_shape=sums_out,
        in_specs=[VM] * 2,
        out_specs=[VM] * 2,
        name="sums1",
    )(came1, node1)
    part0, ship0 = pl.pallas_call(
        sum_kernel,
        out_shape=sums_out,
        in_specs=[VM] * 3,
        out_specs=[VM] * 2,
        name="sums0",
    )(idx, local0, came0)
    lower = lax.ppermute(edge0, "pipe", down)
    upper = lax.ppermute(edge1, "pipe", up)
    edge_final = jnp.where(first, jnp.stack([edge0, lower]), jnp.stack([upper, edge1]))[None]
    r0 = lax.ppermute(ship0, "pipe", down)
    r1 = lax.ppermute(ship1, "pipe", up)
    node_final, we, wem, wn, wnm = pl.pallas_call(
        end_kernel,
        out_shape=[
            shape((1, 2, n_rows, width), BF),
            shape((1, 24, width), F32),
            shape((1, 2, 8, width), F32),
            shape((1, 16, width), F32),
            shape((1, 2, 8, width), F32),
        ],
        in_specs=[SM] + [VM] * 6,
        out_specs=[VM] * 5,
        name="end",
    )(c.reshape(1), part0, part1, ship0, ship1, r0, r1)
    bias = jnp.where(first, part0[76, 0:128], part0[76, 128:256]).reshape(16, 8)
    return (
        node_final,
        edge_final,
        we,
        wem,
        bias[None, 0:4],
        bias[4:5],
        wn,
        wnm,
        bias[None, 5:9],
        bias[9:10],
    )


def solution(mesh):
    dom3 = P("dom", None, None)
    in_specs = (
        P("pipe", None, "dom", None),
        P("pipe", None, "dom", None),
        P(None, "dom", None),
        P(None, "dom", None),
        P("dom"),
        P("dom"),
        P("dom"),
        P("dom"),
        dom3,
        dom3,
        dom3,
        P("pipe", None, None),
        P("pipe", None, None, None),
        P("pipe", None, None),
        P("pipe", None),
        P("pipe", None, None),
        P("pipe", None, None, None),
        P("pipe", None, None),
        P("pipe", None),
    )
    out_specs = (
        P("pipe", None, "dom", None),
        P("pipe", None, "dom", None),
        P("pipe", "dom", None),
        P("pipe", None, "dom", None),
        P("pipe", None, "dom"),
        P("pipe", "dom"),
        P("pipe", "dom", None),
        P("pipe", None, "dom", None),
        P("pipe", None, "dom"),
        P("pipe", "dom"),
    )
    return jax.shard_map(body, mesh=mesh, in_specs=in_specs, out_specs=out_specs, check_vma=False)
```

```python
import functools

import jax
import jax.numpy as jnp
from jax import lax
from jax.experimental import pallas as pl
from jax.experimental.pallas import tpu as pltpu
from jax.sharding import PartitionSpec as P

EPS = 1e-05
BF = jnp.bfloat16
F32 = jnp.float32


def dot(a, b):
    return lax.dot_general(a, b, (((1,), (0,)), ((), ())), preferred_element_type=F32)


def dot_t0(a, b):
    return lax.dot_general(a, b, (((0,), (0,)), ((), ())), preferred_element_type=F32)


def dot_t1(a, b):
    return lax.dot_general(a, b, (((1,), (1,)), ((), ())), preferred_element_type=F32)


def hot_rows(index_row, rows):
    grid = lax.broadcasted_iota(jnp.int32, (rows, index_row.shape[1]), 0)
    return jnp.where(grid == index_row, 1.0, 0.0)


def spread_rows(per, count):
    shape = (8 * per, count * per)
    row = lax.broadcasted_iota(jnp.int32, shape, 0)
    col = lax.broadcasted_iota(jnp.int32, shape, 1)
    return jnp.where(col == (row & 7) * per + (row >> 3), 1.0, 0.0).astype(BF)


def to_chunks(pieces, per):
    count = pieces.shape[0] // per
    rows = dot(spread_rows(per, count), pieces)
    return rows.reshape(per, 8, pieces.shape[1]).astype(BF)


def from_chunks(chunks, count):
    per, _, n = chunks.shape
    rows = chunks.astype(F32).reshape(per * 8, n).astype(BF)
    return dot_t0(spread_rows(per, count), rows).astype(BF)


def fold(rows, per):
    parts = []
    for s in range(rows.shape[0] // per):
        for b in range(rows.shape[1] // 128):
            parts.append(rows[s * per : (s + 1) * per, b * 128 : (b + 1) * 128])
    return jnp.concatenate(parts, axis=0)


def close_rows(pieces, per):
    rows = fold(pieces, per)
    rows = jnp.concatenate([rows, jnp.zeros((4 * per, 128), BF)], axis=0)
    step = 8 * per
    return jnp.concatenate(
        [to_chunks(rows[g * step : (g + 1) * step], per) for g in range(3)], axis=2
    )


def open_rows(chunks, count):
    per = chunks.shape[0]
    parts = [from_chunks(chunks[:, :, g * 128 : (g + 1) * 128], 8) for g in range(3)]
    rows = jnp.concatenate(parts, axis=0)
    step = 4 * per
    return jnp.concatenate(
        [unfold(rows[k * step : (k + 1) * step], per) for k in range(count)], axis=0
    )


def unfold(rows, per):
    return jnp.concatenate([rows[b * per : (b + 1) * per] for b in range(4)], axis=1)


def per_chunk(sums, chunks):
    n = sums.shape[1]
    take = lax.broadcasted_iota(jnp.int32, (128, 16), 0) >> 3
    take = jnp.where(take == lax.broadcasted_iota(jnp.int32, (128, 16), 1), 1.0, 0.0)
    lane = lax.broadcasted_iota(jnp.int32, (128, n), 0)
    col = lax.broadcasted_iota(jnp.int32, (128, n), 1)
    spaced = dot(take.astype(BF), sums.astype(BF))
    spaced = jnp.where((lane & 7) == (col & 7), spaced, 0.0).astype(BF)
    home = lax.broadcasted_iota(jnp.int32, (chunks, n), 1) >> 3
    home = jnp.where(home == lax.broadcasted_iota(jnp.int32, (chunks, n), 0), 1.0, 0.0)
    return dot_t1(home.astype(BF), spaced)


def act(value):
    sig = 0.5 * jnp.tanh(0.5 * value) + 0.5
    out = value * sig
    return out.astype(BF), sig + out * (1.0 - sig)


def norm_rows(value):
    centred = value - jnp.mean(value, axis=-1, keepdims=True)
    inv = lax.rsqrt(jnp.mean(centred * centred, axis=-1, keepdims=True) + EPS)
    return centred * inv, inv


def norm_back(grad, gain, normed, inv):
    scaled = grad * gain
    return inv * (
        scaled
        - jnp.mean(scaled, axis=-1, keepdims=True)
        - normed * jnp.mean(scaled * normed, axis=-1, keepdims=True)
    )


def col_sum(value):
    return jnp.sum(value, axis=0, keepdims=True)


def pre_kernel(
    core, idx, eb, eg, nb, ng, own_all, rec_all, cot_all, out, vec, ownb, recv, cotb, sems
):
    c = core[0]
    cp = [
        pltpu.make_async_copy(own_all.at[0, c], ownb, sems.at[0]),
        pltpu.make_async_copy(cot_all.at[c], cotb, sems.at[1]),
        pltpu.make_async_copy(rec_all.at[0, c], recv, sems.at[2]),
    ]
    for one in cp:
        one.start()
    vec[0:4, :] = eb[0]
    vec[4:5, :] = eg[...]
    vec[5:9, :] = nb[0]
    vec[9:10, :] = ng[...]
    vec[10:16, :] = jnp.zeros((6, vec.shape[1]), F32)
    rows = ownb.shape[0]
    h0, h1, hg = (hot_rows(idx[k : k + 1, :], rows).astype(BF) for k in range(3))
    for one in cp:
        one.wait()
    own, other = ownb[...], recv[...]
    low = jnp.where(c == 0, own.astype(F32), other.astype(F32)).astype(BF)
    top = jnp.where(c == 0, other.astype(F32), own.astype(F32)).astype(BF)
    pairs = ((h0, low), (h1, low), (h0, top), (h1, top), (hg, cotb[...]))
    pieces = jnp.concatenate([dot_t0(hot, src).astype(BF) for hot, src in pairs], axis=0)
    out[...] = close_rows(pieces, idx.shape[1])


def post_kernel(idx, local, came, node_out, hang_out):
    rows = local.shape[0]
    per = came.shape[0]
    total = local[...]
    back = from_chunks(came[...], 8)
    for s in range(2):
        part = unfold(back[s * 4 * per : (s + 1) * 4 * per], per)
        total = total + dot(hot_rows(idx[s : s + 1, :], rows).astype(BF), part)
    low = total.astype(BF)
    node_out[...] = low
    hang = dot_t0(hot_rows(idx[2:3, :], rows).astype(BF), low).astype(BF)
    hang_out[...] = to_chunks(fold(hang, per), per)


def sum_kernel(idx, local, came, part_out, ship):
    per = came.shape[0]
    half = came.shape[2]
    part = jnp.sum(came[...].astype(F32), axis=0)
    part_out[...] = part
    tail = came[:, 72:80, :].astype(F32).reshape(per * 8, half).astype(BF)
    quarters = dot_t0(spread_rows(per, 5), tail).astype(BF)
    rows = local.shape[0]
    total = local[...]
    for s in range(2):
        back = jnp.concatenate(
            [quarters[(s + 2 * k) * per : (s + 2 * k + 1) * per, :] for k in range(2)], axis=1
        )
        total = total + dot(hot_rows(idx[s : s + 1, :], rows).astype(BF), back)
    ship[0:rows, :] = total.astype(BF)
    split_part(part, ship, rows)


def split_part(part, ship, rows):
    high = part.astype(BF)
    low = (part - high.astype(F32)).astype(BF)
    ship[rows:, :] = jnp.concatenate([high, low], axis=1)


def first_kernel(came, node, part_out, ship):
    rows = node.shape[0]
    part = jnp.sum(came[...].astype(F32), axis=0)
    part = jnp.concatenate([part, jnp.zeros((8, part.shape[1]), F32)], axis=0)
    part_out[...] = part
    ship[0:rows, :] = node[...]
    split_part(part, ship, rows)


def end_kernel(core, p0, p1, s0, s1, r0, r1, node_out, we, wem, eb, eg, wn, wnm, nb, ng):
    def part_of(ship):
        rows = node_out.shape[2]
        half = p0.shape[1]
        return ship[rows:, :half].astype(F32) + ship[rows:, half:].astype(F32)

    def write(left, right, first, second, sums):
        for v in range(4):
            eb[0, v : v + 1, :] = sums[:, v * 8 : v * 8 + 8]
            nb[0, v : v + 1, :] = sums[:, v * 8 + 40 : v * 8 + 48]
        eg[...] = sums[:, 32:40]
        ng[...] = sums[:, 72:80]
        full = jnp.concatenate([left, right], axis=1)
        rows = node_out.shape[2]
        node_out[0, 0] = first[0:rows, :]
        node_out[0, 1] = second[0:rows, :]
        we[0] = full[0:24, :]
        wem[0, 0] = full[24:32, :]
        wem[0, 1] = full[64:72, :]
        wn[0] = full[32:48, :]
        wnm[0, 0] = full[48:56, :]
        wnm[0, 1] = full[56:64, :]

    @pl.when(core[0] == 0)
    def _():
        write(p0[...], part_of(r0), s0, r0, p0[76:77, 0:128])

    @pl.when(core[0] == 1)
    def _():
        write(part_of(r1), p1[...], r1, s1, p0[76:77, 128:256])


SAVED = 7


def unit_kernel(mode, *refs):
    take = iter(refs)

    def some(n):
        return [next(take) for _ in range(n)]

    scal, idx, erow, got = some(4)
    per = idx.shape[1]
    hang_in = next(take) if mode == 0 else None
    own_nodes, own_edges, *own_rest = some(7)
    recs = some(7)
    gout_all, gedge_all = some(2)
    bias_in = next(take) if mode == 0 else None
    local_ref, edge_out, keep_out, send_out = some(4)
    back_ref, bias_ref, inc_out = some(3) if mode == 1 else (None, None, None)
    dsts = some(7)
    nodes, edges, w1, wm, n1, nm, vec = dsts
    saved = some(SAVED)
    oh, a1, a2, s1, s2, nrm, inv = saved
    q, msg, gout, gedge, l1, l2, l3, gag, bsum, inc = some(10)
    edge_ref, left_ref, right_ref = some(3)
    sems = next(take)
    sent = []


    is_own, c, node_count, edge_count, gi = (scal[i] for i in range(5))
    owns = [own_nodes.at[0, c], own_edges.at[0, c]] + [r.at[0] for r in own_rest[:4]]
    owns = owns + [own_rest[4]]
    recs = [recs[0].at[0, c], recs[1].at[0, c]] + recs[2:]
    cg = pltpu.make_async_copy(gout_all.at[gi], gout, sems.at[7])
    ce = pltpu.make_async_copy(gedge_all.at[gi], gedge, sems.at[8])

    def fetch(order):
        @pl.when(is_own == 1)
        def _():
            for k in order:
                pltpu.make_async_copy(owns[k], dsts[k], sems.at[k]).start()

        @pl.when(is_own == 0)
        def _():
            for k in order:
                pltpu.make_async_copy(recs[k], dsts[k], sems.at[k]).start()

    fetch([6, 0, 2, 1, 3])

    def ready(k):
        pltpu.make_async_copy(recs[k], dsts[k], sems.at[k]).wait()

    n_rows = nodes.shape[0]
    e_rows = edges.shape[0]
    width = nodes.shape[1]
    block = e_rows
    blocks = e_rows // block

    def live_of(start, size, count):
        return (lax.broadcasted_iota(jnp.int32, (size, 1), 0) + start < count).astype(F32)

    ready(6)
    eb = [vec[i : i + 1, :] for i in range(4)]
    eg = vec[4:5, :]
    nb = [vec[i : i + 1, :] for i in range(5, 9)]
    ng = vec[9:10, :]
    to_target = hot_rows(erow[1:2, :], n_rows).astype(BF)

    if mode == 1:
        pieces = open_rows(got[...], 5)
        inc_out[...] = pieces[0 : 2 * per]
        inc[...] = pieces[2 * per : 4 * per]
        from_hanging = pieces[4 * per :]
    else:
        inc[...] = got[...]
        from_hanging = unfold(from_chunks(hang_in[...], 4), per)

    ecol = jnp.transpose(erow[...])
    grid = lax.broadcasted_iota(jnp.int32, (e_rows, width), 1)
    hit = (grid == ecol[:, 0:1]) | (grid == ecol[:, 1:2])
    oh[...] = jnp.where(hit, 1.0, 0.0).astype(BF)
    ready(0)
    ready(2)
    q[0:n_rows, :] = dot(nodes[...], w1[width : 2 * width, :]).astype(BF)
    q[n_rows : 2 * n_rows, :] = dot(nodes[...], w1[0:width, :]).astype(BF)
    q[2 * n_rows :, :] = dot(inc[...], w1[0:width, :]).astype(BF)
    ready(1)
    ready(3)
    fetch([4, 5])
    cg.start()
    ce.start()

    def forward(i, _):
        start = pl.multiple_of(i * block, block)
        rows = pl.ds(start, block)
        z = dot(oh[rows, :], q[...]) + dot(edges[rows, :], w1[2 * width :, :]) + eb[0]
        low, slope = act(z)
        a1[rows, :] = low
        s1[rows, :] = slope
        low, slope = act(dot(low, wm[0]) + eb[1])
        a2[rows, :] = low
        s2[rows, :] = slope
        normed, rstd = norm_rows(dot(low, wm[1]) + eb[2])
        nrm[rows, :] = normed
        inv[rows, :] = jnp.broadcast_to(rstd, (block, 128))
        msg[rows, :] = ((normed * eg + eb[3]) * live_of(start, block, edge_count)).astype(BF)
        return 0

    lax.fori_loop(0, blocks, forward, 0)

    agg = dot(to_target, msg[...]).astype(BF)
    ready(4)
    ready(5)
    x_n = nodes[...]
    na1, ns1 = act(dot(x_n, n1[0:width, :]) + dot(agg, n1[width:, :]) + nb[0])
    na2, ns2 = act(dot(na1, nm[0]) + nb[1])
    nn, nr = norm_rows(dot(na2, nm[1]) + nb[2])
    nr = jnp.broadcast_to(nr, (n_rows, 128))


    def put(first, pieces):
        half = width // 2
        tile = jnp.concatenate([x.reshape(64, -1, x.shape[-1]) for x in pieces], axis=1)
        n = tile.shape[1]
        left_ref[:, first : first + n, :] = tile[:, :, :half].astype(BF)
        right_ref[:, first : first + n, :] = tile[:, :, half:].astype(BF)
        part = (slice(None), pl.ds(first, n), slice(None))

        def copies(one, two):
            return [
                pltpu.make_async_copy(ref.at[part], out.at[part], sems.at[24 + len(sent) * 2 + k])
                for k, (ref, out) in enumerate(((two, send_out), (one, keep_out)))
            ]

        @pl.when(c == 0)
        def _():
            for copy in copies(left_ref, right_ref):
                copy.start()

        @pl.when(c == 1)
        def _():
            for copy in copies(right_ref, left_ref):
                copy.start()

        sent.append(copies(left_ref, right_ref))

    cg.wait()
    hung = jnp.max(
        jnp.where(
            lax.broadcasted_iota(jnp.int32, (n_rows, idx.shape[1]), 0) == idx[2:3, :], 1.0, 0.0
        ),
        axis=1,
        keepdims=True,
    )
    spread = 0.5 * (hot_rows(idx[3:4, :], n_rows) + hot_rows(idx[4:5, :], n_rows))
    grad_new = gout[...].astype(F32) * (1.0 - hung) + dot(spread.astype(BF), from_hanging)
    gy = grad_new * live_of(0, n_rows, node_count)
    bsum[8:9, :] = col_sum(gy)
    bsum[9:10, :] = col_sum(gy * nn)
    g3 = norm_back(gy, ng, nn, nr[:, 0:1])
    bsum[7:8, :] = col_sum(g3)
    low3 = g3.astype(BF)
    g2 = dot_t1(low3, nm[1]) * ns2
    bsum[6:7, :] = col_sum(g2)
    low2 = g2.astype(BF)
    g1 = dot_t1(low2, nm[0]) * ns1
    bsum[5:6, :] = col_sum(g1)
    low1 = g1.astype(BF)
    direct = grad_new + dot_t1(low1, n1[0:width, :])
    gag[0:n_rows, :] = dot_t1(low1, n1[width:, :]).astype(BF)
    gag[n_rows:, :] = jnp.zeros((gag.shape[0] - n_rows, width), BF)
    put(32, [jnp.concatenate([dot_t0(x_n, low1), dot_t0(agg, low1)], axis=0)])
    put(48, [dot_t0(na1, low2), dot_t0(na2, low3)])

    ce.wait()
    gk = gag.shape[0]

    def backward(i, carry):
        start = pl.multiple_of(i * block, block)
        rows = pl.ds(start, block)
        c1, c2, c3, c4, c5 = carry
        ge = gedge[rows, :].astype(F32)
        gy = (dot(oh[rows, 0:gk], gag[...]) + ge) * live_of(start, block, edge_count)
        normed = nrm[rows, :]
        g3 = norm_back(gy, eg, normed, inv[rows, 0:1])
        low = g3.astype(BF)
        l3[rows, :] = low
        g2 = dot_t1(low, wm[1]) * s2[rows, :]
        low = g2.astype(BF)
        l2[rows, :] = low
        g1 = dot_t1(low, wm[0]) * s1[rows, :]
        low = g1.astype(BF)
        l1[rows, :] = low
        edge_ref[rows, :] = (ge + dot_t1(low, w1[2 * width :, :])).astype(BF)
        pltpu.make_async_copy(edge_ref.at[rows, :], edge_out.at[rows, :], sems.at[23]).start()
        return (
            c1 + col_sum(g1),
            c2 + col_sum(g2),
            c3 + col_sum(g3),
            c4 + col_sum(gy),
            c5 + col_sum(gy * normed),
        )

    zero = jnp.zeros((1, width), F32)
    sums = lax.fori_loop(0, blocks, backward, (zero,) * 5)
    for k in range(5):
        bsum[k : k + 1, :] = sums[k]
    bsum[10:16, :] = jnp.zeros((6, width), F32)

    lowv = l1[...]
    t_sum = dot(to_target, lowv).astype(BF)
    from_source = hot_rows(erow[0:1, :] - n_rows, width - n_rows).astype(BF)
    s_sum = dot(from_source, lowv).astype(BF)
    d_ext = dot_t1(s_sum, w1[0:width, :])
    local_ref[...] = direct + d_ext[0:n_rows, :] + dot_t1(t_sum, w1[width : 2 * width, :])
    d_inc = d_ext[n_rows:, :].astype(BF)
    bias_row = per_chunk(bsum[...], per)
    half = width // 2
    extra = []
    if mode == 1:
        back_ref[...] = to_chunks(fold(d_inc, per), per)
        bias_ref[...] = bias_row
    else:
        bias_row = jnp.concatenate([bias_row, bias_in[...]], axis=1).astype(BF)
        kept = jnp.concatenate([d_inc[:, :half], d_inc[:, half:], bias_row], axis=0)
        given = jnp.concatenate([jnp.zeros((4 * per, half), BF), bias_row], axis=0)
        one = jnp.where(c == 0, kept.astype(F32), given.astype(F32)).astype(BF)
        two = jnp.where(c == 0, given.astype(F32), kept.astype(F32)).astype(BF)
        place = spread_rows(per, 5)
        extra = [jnp.concatenate([dot(place, one), dot(place, two)], axis=1)]
    put(64, [dot_t0(a2[...], l3[...])] + extra)
    grad_w1 = jnp.concatenate(
        [
            dot_t0(x_n, s_sum[0:n_rows, :]) + dot_t0(inc[...], s_sum[n_rows:, :]),
            dot_t0(x_n, t_sum),
            dot_t0(edges[...], lowv),
        ],
        axis=0,
    )
    put(0, [grad_w1, dot_t0(a1[...], l2[...])])
    for pair in sent:
        for copy in pair:
            copy.wait()
    pltpu.make_async_copy(edge_ref, edge_out, sems.at[23]).wait()


VM = pl.BlockSpec(memory_space=pltpu.VMEM)
SM = pl.BlockSpec(memory_space=pltpu.SMEM)
HB = pl.BlockSpec(memory_space=pl.ANY)


def swap(x):
    return lax.ppermute(x, "pipe", [(0, 1), (1, 0)])


def exchange(x):
    return lax.all_to_all(x, "dom", split_axis=0, concat_axis=0, tiled=True)


def body(
    node_in, edge_in, cot_node, cot_edge, node_count, edge_count, edge_source, edge_target,
    halo_send, hang_send, parent_rows,
    w_edge_in, w_edge_mid, edge_bias, edge_gain, w_node_in, w_node_mid, node_bias, node_gain,
):
    n_rows, width = node_in.shape[2:]
    e_rows = edge_in.shape[2]
    peers = lax.axis_size("dom")
    slots = halo_send.shape[2]
    c = lax.axis_index("pipe")
    half = width // 2

    rec_nodes = swap(node_in)

    hs, gs, ps = halo_send[0], hang_send[0], parent_rows[0]
    idx = jnp.stack([hs[:, 0], hs[:, 1], gs[:, 0], ps[:, 0], ps[:, 1]] + [hs[:, 0]] * 3)
    rec_nodes, idx = lax.optimization_barrier((rec_nodes, idx))
    outs, vec = pl.pallas_call(
        pre_kernel,
        out_shape=[
            jax.ShapeDtypeStruct((peers, 8, 384), BF),
            jax.ShapeDtypeStruct((16, width), F32),
        ],
        in_specs=[SM] + [VM] * 5 + [HB] * 3,
        out_specs=[VM] * 2,
        scratch_shapes=[pltpu.VMEM((n_rows, width), BF)] * 3 + [pltpu.SemaphoreType.DMA((3,))],
        name="pre",
    )(
        c.reshape(1), idx, edge_bias, edge_gain, node_bias, node_gain,
        node_in, rec_nodes, cot_node,
    )
    rec_vec = swap(vec)
    bulk = (edge_in, w_edge_in, w_edge_mid, w_node_in, w_node_mid)
    bulk, _ = lax.optimization_barrier((bulk, rec_nodes))
    rec_edges = swap(bulk[0])
    rec_w1, rec_wm, rec_n1, rec_nm = (swap(w[0]) for w in bulk[1:])
    bulk = (rec_edges, rec_w1, rec_wm, rec_n1, rec_nm, edge_source, edge_target)
    bulk = lax.optimization_barrier(bulk)
    rec_edges, rec_w1, rec_wm, rec_n1, rec_nm, edge_source, edge_target = bulk
    k = edge_source - n_rows
    source = jnp.where(k < 0, edge_source, n_rows + (k % slots) * peers + k // slots)
    erow = jnp.stack([n_rows + source, edge_target] + [edge_target] * 6, axis=0)

    got = exchange(outs)

    shape = jax.ShapeDtypeStruct
    saved = [shape((e_rows, width), BF)] * 3 + [shape((e_rows, width), F32)] * 3
    saved += [shape((e_rows, 128), F32)]

    def results(mode):
        chunk = shape((peers, 72 if mode == 1 else 80, half), BF)
        some = [shape((n_rows, width), F32), shape((e_rows, width), BF), chunk, chunk]
        if mode == 1:
            some += [shape((peers, 8, 128), BF), shape((peers, 128), F32)]
            some += [shape((slots * peers, width), BF)]
        return some

    stages = [
        shape((n_rows, width), BF),
        shape((e_rows, width), BF),
        shape(w_edge_in.shape[1:], BF),
        shape(w_edge_mid.shape[1:], BF),
        shape(w_node_in.shape[1:], BF),
        shape(w_node_mid.shape[1:], BF),
        shape((16, width), F32),
    ]
    work = [
        shape((width, width), BF),
        shape((e_rows, width), BF),
        shape((n_rows, width), BF),
        shape((e_rows, width), BF),
        shape((e_rows, width), BF),
        shape((e_rows, width), BF),
        shape((e_rows, width), BF),
        shape((256, width), BF),
        shape((16, width), F32),
        shape((slots * peers, width), BF),
    ]

    def run(layer, got, gout, gedge, gi, hang_l=(), bias=()):
        own = (c == layer).astype(jnp.int32)
        scal = jnp.stack([own, c, node_count[0], edge_count[0], jnp.int32(gi)]).astype(jnp.int32)
        arrays = [scal, idx, erow, got] + list(hang_l)
        near = len(arrays) - 1
        arrays += [node_in, edge_in, w_edge_in, w_edge_mid, w_node_in, w_node_mid, vec]
        arrays += [rec_nodes, rec_edges, rec_w1, rec_wm, rec_n1, rec_nm, rec_vec]
        arrays += [gout, gedge]
        far = len(arrays)
        arrays += list(bias)
        outs = results(layer)
        return pl.pallas_call(
            functools.partial(unit_kernel, layer),
            out_shape=outs,
            in_specs=[SM] + [VM] * near + [HB] * (far - near - 1) + [VM] * len(bias),
            out_specs=[VM, HB, HB, HB] + [VM] * (len(outs) - 4),
            scratch_shapes=[pltpu.VMEM(x.shape, x.dtype) for x in stages + saved + work + outs[1:4]]
            + [pltpu.SemaphoreType.DMA((40,))],
            compiler_params=pltpu.CompilerParams(vmem_limit_bytes=60 * 1024 * 1024),
        )(*arrays)

    post = pl.pallas_call(
        post_kernel,
        out_shape=[shape((n_rows, width), BF), shape((peers, 8, 128), BF)],
        in_specs=[VM] * 3,
        out_specs=[VM] * 2,
        name="post",
    )

    def paired(keep, send):
        return (keep.astype(F32) + swap(send).astype(F32)).astype(BF)

    local1, edge1, keep1, send1, back1, bias1, inc0 = run(1, got, cot_node, cot_edge, c)
    node1, hang1 = post(idx, local1, exchange(back1))
    hang_in0 = exchange(hang1)
    mine1, hang_in0 = lax.optimization_barrier((paired(keep1, send1), hang_in0))
    came1 = exchange(mine1)
    local0, edge0, keep0, send0 = run(
        0, inc0, node1[None], edge1[None], 0, [hang_in0], [bias1]
    )
    up = [(0, 1)]
    down = [(1, 0)]
    first = c == 0
    came0 = exchange(paired(keep0, send0))
    sums_out = [shape((80, half), F32), shape((n_rows + 80, width), BF)]
    part1, ship1 = pl.pallas_call(
        first_kernel,
        out_shape=sums_out,
        in_specs=[VM] * 2,
        out_specs=[VM] * 2,
        name="sums1",
    )(came1, node1)
    part0, ship0 = pl.pallas_call(
        sum_kernel,
        out_shape=sums_out,
        in_specs=[VM] * 3,
        out_specs=[VM] * 2,
        name="sums0",
    )(idx, local0, came0)
    lower = lax.ppermute(edge0, "pipe", down)
    upper = lax.ppermute(edge1, "pipe", up)
    edge_final = jnp.where(first, jnp.stack([edge0, lower]), jnp.stack([upper, edge1]))[None]
    r0 = lax.ppermute(ship0, "pipe", down)
    r1 = lax.ppermute(ship1, "pipe", up)
    ends = pl.pallas_call(
        end_kernel,
        out_shape=[
            shape((1, 2, n_rows, width), BF),
            shape((1, 24, width), F32),
            shape((1, 2, 8, width), F32),
            shape((1, 4, 8), F32),
            shape((1, 8), F32),
            shape((1, 16, width), F32),
            shape((1, 2, 8, width), F32),
            shape((1, 4, 8), F32),
            shape((1, 8), F32),
        ],
        in_specs=[SM] + [VM] * 6,
        out_specs=[VM] * 9,
        name="end",
    )(c.reshape(1), part0, part1, ship0, ship1, r0, r1)
    return (ends[0], edge_final, *ends[1:])


def solution(mesh):
    dom3 = P("dom", None, None)
    in_specs = (
        P("pipe", None, "dom", None),
        P("pipe", None, "dom", None),
        P(None, "dom", None),
        P(None, "dom", None),
        P("dom"),
        P("dom"),
        P("dom"),
        P("dom"),
        dom3,
        dom3,
        dom3,
        P("pipe", None, None),
        P("pipe", None, None, None),
        P("pipe", None, None),
        P("pipe", None),
        P("pipe", None, None),
        P("pipe", None, None, None),
        P("pipe", None, None),
        P("pipe", None),
    )
    out_specs = (
        P("pipe", None, "dom", None),
        P("pipe", None, "dom", None),
        P("pipe", "dom", None),
        P("pipe", None, "dom", None),
        P("pipe", None, "dom"),
        P("pipe", "dom"),
        P("pipe", "dom", None),
        P("pipe", None, "dom", None),
        P("pipe", None, "dom"),
        P("pipe", "dom"),
    )
    return jax.shard_map(body, mesh=mesh, in_specs=in_specs, out_specs=out_specs, check_vma=False)
```
